128 devices in a mesh: gx: 16 (over x, z), gy: 8 (over y, core).
Axes of the slice: x: 4, y: 4, z: 4, core: 2. Of those that a mesh axis runs over, the one named last changes fastest.
Arguments:
- control: float32 [2, 32, 512, 2048], P(None, None, 'gx', 'gy'), may hold values from -6 to 6
- band_roots: float32 [16, 32, 32], replicated, may hold values from -1 to 1
Outputs:
- increment: float32 [2, 32, 512, 2048], P(None, None, 'gx', 'gy')
The draws below stay inside these ranges and needn't reach their ends.
All inputs are finite; a program needn't handle non-finite values.
Results may differ from the reference program's by a relative error of at most 0.000053.
Values sent between devices are 32-bit elements; how exact they have to be, the bound alone decides.
A program may use at most 64 MiB of HBM per device.

```python
import jax
import jax.numpy as jnp
from jax import lax

L = 32
LEVELS = 5
BANDS = 16
NV = 2
NX = 512
NY = 2048


def block_scale(key, extent, cuts, least, largest):
    def one(position, shards_of):
        draws = jax.random.uniform(jax.random.fold_in(jax.random.fold_in(key, 6), position), (shards_of,), jnp.float32, least / len(cuts), largest / len(cuts))
        return jnp.repeat(jnp.exp(draws), extent[position] // shards_of).reshape((-1,) + (1,) * (len(extent) - position - 1))

    factor_of = one(*cuts[0])
    for cut in cuts[1:]:
        factor_of = factor_of * one(*cut)
    return factor_of


def bell_draw(key, shape, scale, most, shards=(), kind=jnp.bfloat16):
    loudness = block_scale(key, shape, shards, -0.22, 0.18) if shards else 1.0
    drawn = jax.random.normal(key, shape, jnp.float32) * scale * loudness
    return jnp.minimum(jnp.maximum(drawn, -most), most).astype(kind)


def setup_inputs(seed: int = 0) -> dict:
    keys = jax.random.split(jax.random.key(seed), 3)
    return {
        "control": bell_draw(keys[0], (NV, L, NX, NY), 1.0, 6.0, ((2, 16), (3, 8)), jnp.float32),
        "band_roots": bell_draw(keys[1], (BANDS, L, L), L ** -0.5, 1.0, (), jnp.float32),
    }


def slab_of(source, begin_at, end_at, stride, dimension):
    return lax.slice_in_dim(source, begin_at, end_at, stride, dimension)


def alternate(even_part, odd_part, dimension):
    joined = jnp.stack([even_part, odd_part], dimension + 1)
    shape_out = list(even_part.shape)
    shape_out[dimension] = shape_out[dimension] * 2
    return joined.reshape(shape_out)


def forward_lift(signal, dimension):
    length = signal.shape[dimension]
    half_len = length // 2
    even_part = slab_of(signal, 0, length, 2, dimension)
    odd_part = slab_of(signal, 1, length, 2, dimension)
    edge = jnp.zeros_like(slab_of(even_part, 0, 1, 1, dimension))
    after_part = jnp.concatenate([slab_of(even_part, 1, half_len, 1, dimension), edge], dimension)
    detail = odd_part - 0.5 * (even_part + after_part)
    before = jnp.concatenate([edge, slab_of(detail, 0, half_len - 1, 1, dimension)], dimension)
    smooth = even_part + 0.25 * (before + detail)
    return smooth, detail


def inverse_lift(smooth, detail, dimension):
    half_len = smooth.shape[dimension]
    edge = jnp.zeros_like(slab_of(detail, 0, 1, 1, dimension))
    before = jnp.concatenate([edge, slab_of(detail, 0, half_len - 1, 1, dimension)], dimension)
    even_part = smooth - 0.25 * (before + detail)
    after_part = jnp.concatenate([slab_of(even_part, 1, half_len, 1, dimension), edge], dimension)
    odd_part = detail + 0.5 * (even_part + after_part)
    return alternate(even_part, odd_part, dimension)


def vertical(band_roots, band_index, coeffs):
    return jnp.einsum("lm,nmxy->nlxy", band_roots[band_index], coeffs, precision=lax.Precision.HIGHEST)


def analyse(signal):
    vectors = signal.shape[0]
    smooth, detail = forward_lift(signal, 2)
    stacked = jnp.concatenate([smooth, detail], 0)
    upper, lower = forward_lift(stacked, 3)
    return upper[:vectors], (lower[:vectors], upper[vectors:], lower[vectors:])


def synthesise(coarse, band_list):
    vectors = coarse.shape[0]
    rows_smooth = jnp.concatenate([coarse, band_list[1]], 0)
    rows_detail = jnp.concatenate([band_list[0], band_list[2]], 0)
    both = inverse_lift(rows_smooth, rows_detail, 3)
    return inverse_lift(both[:vectors], both[vectors:], 2)


def reference(control, band_roots):
    def descend(signal, level_now):
        if level_now == LEVELS:
            return vertical(band_roots, 3 * LEVELS, signal)
        coarse, band_list = analyse(signal)
        band_list = tuple(vertical(band_roots, 3 * level_now + offset, member) for offset, member in enumerate(band_list))
        return synthesise(descend(coarse, level_now + 1), band_list)

    return descend(control, 0)
```

```python
from functools import partial

import jax
import jax.numpy as jnp
from jax import lax
from jax.experimental import pallas as pl
from jax.experimental.pallas import tpu as pltpu
from jax.sharding import PartitionSpec as P

LEVELS = 5
F32 = jnp.float32
BF16 = jnp.bfloat16


def round_up(value, step):
    return (value + step - 1) // step * step


class Level:
    def __init__(self, planes, rows):
        self.n = planes
        self.y = rows
        self.h = planes // 2
        self.hy = rows // 2
        self.r = round_up(rows + 16, 16)
        self.rb = round_up(self.hy + 16, 16)
        self.npad = max(planes, 8)
        self.short = planes < 3
        self.sent = self.npad + 16
        self.got = self.npad + 24


def levels_of(planes, rows):
    return [Level(planes >> k, rows >> k) for k in range(LEVELS)]


def each(count, body, unroll_to=4):
    if count <= unroll_to:
        for i in range(count):
            body(i)
    else:

        @pl.loop(0, count)
        def _(i):
            body(i)


def kernel(levels, counts, x_hbm, w_ref, out_ref, *scratch):
    count_x, count_y = counts
    (xin, mats, in_sem, send_sem, recv_sem) = scratch[:5]
    per = scratch[5:]
    width = 11
    lv_refs = [per[k * width : (k + 1) * width] for k in range(LEVELS)]
    gx = lax.axis_index("gx")
    gy = lax.axis_index("gy")
    first_x, last_x = gx == 0, gx == count_x - 1
    planes_in = levels[0].n
    rows_in = levels[0].y
    cells = xin.shape[1] // planes_in

    def at(dx, dy):
        return {
            "gx": lax.rem(gx + dx + count_x, count_x),
            "gy": lax.rem(gy + dy + count_y, count_y),
        }

    friends = [
        (dx, dy) for dx in (-2, -1, 0, 1, 2) for dy in (-1, 0, 1) if (dx, dy) != (0, 0)
    ]
    barrier = pltpu.get_barrier_semaphore()
    for dx, dy in friends:
        pl.semaphore_signal(
            barrier, inc=1, device_id=at(dx, dy), device_id_type=pl.DeviceIdType.MESH
        )

    loads = [
        pltpu.make_async_copy(
            x_hbm.at[:, side * rows_in : (side + 1) * rows_in], xin.at[side], in_sem.at[side]
        )
        for side in range(2)
    ]
    for load in loads:
        load.start()

    lane = lax.broadcasted_iota(jnp.int32, (1, 128), 1)
    upper = lane >= 64
    keep_next = jnp.logical_or(lane < 64, gy < count_y - 1)
    keep_prev = jnp.logical_or(lane >= 64, gy > 0)

    block_row = lax.broadcasted_iota(jnp.int32, (128, 128), 0) // 32
    block_lane = lax.broadcasted_iota(jnp.int32, (128, 128), 1) // 32
    diagonal = block_row == block_lane

    def build(band):
        small = jnp.concatenate([w_ref[band]] * 4, axis=1)
        tiled = jnp.concatenate([small] * 4, axis=0)
        square = jnp.where(diagonal, tiled, 0.0).T
        high = square.astype(BF16)
        low = (square - high.astype(F32)).astype(BF16)
        mats[band, 0:128, 0:128] = high
        mats[band, 128:256, 0:128] = high
        mats[band, 0:128, 128:256] = low
        mats[band, 128:256, 128:256] = jnp.zeros((128, 128), BF16)

    each(16, build)

    for load in loads:
        load.wait()

    def take(x):
        low = xin[0, pl.ds(x, cells, stride=planes_in), :]
        high = xin[1, pl.ds(x, cells, stride=planes_in), :]
        tile = jnp.concatenate([low, high], axis=0)
        lv_refs[0][0][x + 1, 8 : 8 + rows_in, :] = tile.T

    each(planes_in, take)

    pl.semaphore_wait(barrier, len(friends))

    def copies(k):
        lv = levels[k]
        a, sp, en, es, rn, rs = lv_refs[k][:6]
        rows = pl.ds(8, lv.y)
        moves = [
            (a.at[1, rows], a.at[lv.n + 1, rows], (-1, 0)),
            (a.at[2, rows] if lv.short else sp.at[0], a.at[lv.n + 2, rows], (-1, 0)),
            (sp.at[1], a.at[0, rows], (1, 0)),
        ]
        if lv.short:
            moves.append((a.at[1, rows], a.at[lv.n + 3, rows], (-2, 0)))
        groups = [
            (pl.ds(0, lv.npad), pl.ds(0, lv.npad), 0),
            (pl.ds(lv.npad, 8), pl.ds(lv.npad, 8), -1),
            (pl.ds(lv.npad + 8, 8), pl.ds(lv.npad + 8, 8), 1),
        ]
        if lv.short:
            groups.append((pl.ds(lv.npad, 8), pl.ds(lv.npad + 16, 8), -2))
        for source, target, dx in groups:
            moves.append((en.at[:, source], rn.at[:, target], (dx, -1)))
            moves.append((es.at[:, source], rs.at[:, target], (dx, 1)))
        return [
            pltpu.make_async_remote_copy(
                src_ref=source,
                dst_ref=target,
                send_sem=send_sem.at[k, m],
                recv_sem=recv_sem.at[k, m],
                device_id=at(*way),
                device_id_type=pl.DeviceIdType.MESH,
            )
            for m, (source, target, way) in enumerate(moves)
        ]

    def send(k):
        lv = levels[k]
        a, sp, en, es = lv_refs[k][:4]
        n, y = lv.n, lv.y
        todo = copies(k)
        rows = pl.ds(8, y)
        if not lv.short:
            sp[0] = a[2, rows] - 0.5 * (a[1, rows] + a[3, rows])
        sp[1] = a[n, rows] - 0.5 * a[n - 1, rows]
        x_moves = 4 if lv.short else 3
        for copy in todo[:x_moves]:
            copy.start()

        def edge(x):
            one = pl.ds(x, 1)
            r0, r1, r2 = a[x + 1, 8:9], a[x + 1, 9:10], a[x + 1, 10:11]
            before, end = a[x + 1, y + 6 : y + 7], a[x + 1, y + 7 : y + 8]
            en[0, one] = r0
            en[1, one] = r1 - 0.5 * (r0 + r2)
            es[0, one] = end - 0.5 * before

        each(n, edge, 8)
        for ref, kinds in ((en, 2), (es, 1)):
            for kind in range(kinds):
                row = lambda i: ref[kind, i : i + 1]
                ref[kind, lv.npad : lv.npad + 1] = row(0)
                second = row(1) if lv.short else row(1) - 0.5 * (row(0) + row(2))
                ref[kind, lv.npad + 1 : lv.npad + 2] = second
                ref[kind, lv.npad + 8 : lv.npad + 9] = row(n - 1) - 0.5 * row(n - 2)
        for copy in todo[x_moves:]:
            copy.start()

    def receive(k):
        for copy in copies(k):
            copy.wait_recv()

    def fill(k):
        lv = levels[k]
        a, sp, en, es, rn, rs = lv_refs[k][:6]
        n, y = lv.n, lv.y

        def place(plane, f_here, d_here, q_here, slot):
            f_there, d_there, q_there = rn[0, slot], rn[1, slot], rs[0, slot]
            turn = lambda value: pltpu.roll(value, 64, 1)
            a[plane, y + 8 : y + 9] = jnp.where(
                keep_next, turn(jnp.where(upper, f_here, f_there)), 0.0
            )
            a[plane, y + 9 : y + 10] = jnp.where(
                keep_next, turn(jnp.where(upper, d_here, d_there)), 0.0
            )
            a[plane, 7:8] = turn(jnp.where(upper, q_there, q_here))

        def local(x):
            one = pl.ds(x, 1)
            place(x + 1, en[0, one], en[1, one], es[0, one], one)

        each(n, local, 8)
        halo = [(n + 1, lv.npad), (n + 2, lv.npad + 1), (0, lv.npad + 8)]
        if lv.short:
            halo.append((n + 3, lv.npad + 16))
        for plane, slot in halo:
            r0, r1, r2 = a[plane, 8:9], a[plane, 9:10], a[plane, 10:11]
            before, end = a[plane, y + 6 : y + 7], a[plane, y + 7 : y + 8]
            place(plane, r0, r1 - 0.5 * (r0 + r2), end - 0.5 * before, pl.ds(slot, 1))
        if lv.short:

            @pl.when(gx == count_x - 2)
            def _():
                a[n + 3] = jnp.zeros_like(a[n + 3])

            a[n + 2] = a[n + 2] - 0.5 * (a[n + 1] + a[n + 3])

        @pl.when(last_x)
        def _():
            a[n + 1] = jnp.zeros_like(a[n + 1])
            a[n + 2] = jnp.zeros_like(a[n + 2])

        @pl.when(first_x)
        def _():
            a[0] = 0.5 * a[1]

    def lift_x(k):
        lv = levels[k]
        a, sx, dx = lv_refs[k][0], lv_refs[k][6], lv_refs[k][7]
        n, h = lv.n, lv.h
        dx[0] = a[0] - 0.5 * a[1]

        def step(i):
            even = a[2 * i + 1]
            detail = a[2 * i + 2] - 0.5 * (even + a[2 * i + 3])
            dx[i + 1] = detail
            sx[i] = even + 0.25 * (dx[i] + detail)

        each(h, step)
        dx[h + 1] = a[n + 2]
        sx[h] = a[n + 1] + 0.25 * (dx[h] + dx[h + 1])

    def lift_y(lv, plane, smooth, detail):
        hy, y = lv.hy, lv.y
        even = plane[pl.ds(8, hy, stride=2), :]
        odd = plane[pl.ds(9, hy, stride=2), :]
        after = plane[pl.ds(10, hy, stride=2), :]
        fresh = odd - 0.5 * (even + after)
        detail[8 : 8 + hy] = fresh
        detail[7:8] = jnp.where(keep_prev, plane[7:8] - 0.5 * plane[8:9], 0.0)
        detail[8 + hy : 9 + hy] = plane[y + 9 : y + 10]
        if smooth is None:
            return
        smooth[8 : 8 + hy] = even + 0.25 * (detail[7 : 7 + hy] + fresh)
        smooth[8 + hy : 9 + hy] = plane[y + 8 : y + 9] + 0.25 * (
            detail[7 + hy : 8 + hy] + detail[8 + hy : 9 + hy]
        )

    def lift_smooth(k):
        lv = levels[k]
        sx, b0 = lv_refs[k][6], lv_refs[k][8]
        coarse = lv_refs[k + 1][0] if k + 1 < LEVELS else None
        if coarse is None:
            target = mats_s5

            def step(i):
                lift_y(lv, sx.at[i], target.at[i], b0.at[i])

            each(lv.h + 1, step)
        else:

            def step(i):
                lift_y(lv, sx.at[i], coarse.at[i + 1], b0.at[i])

            each(lv.h, step)
            lift_y(lv, sx.at[lv.h], None, b0.at[lv.h])

    def lift_detail(k):
        lv = levels[k]
        dx, b1, b2 = lv_refs[k][7], lv_refs[k][9], lv_refs[k][10]

        def step(i):
            lift_y(lv, dx.at[i], b1.at[i], b2.at[i])

        each(lv.h + 2, step)

    def weigh(ref, i, band):
        value = ref[i]
        high = value.astype(BF16)
        low = (value - high.astype(F32)).astype(BF16)
        both = jnp.concatenate([high, low], axis=1)
        product = jnp.dot(both, mats[band], preferred_element_type=F32)
        ref[i] = product[:, :128] + product[:, 128:]

    def weigh_bands(k):
        lv = levels[k]
        b0, b1, b2 = lv_refs[k][8:11]
        each(lv.h + 1, lambda i: weigh(b0, i, 3 * k))
        each(lv.h + 2, lambda i: weigh(b1, i, 3 * k + 1))
        each(lv.h + 2, lambda i: weigh(b2, i, 3 * k + 2))

    def unlift_y(lv, smooth, detail, plane):
        hy, y = lv.hy, lv.y
        fresh = detail[8 : 8 + hy]
        even = smooth[8 : 8 + hy] - 0.25 * (detail[7 : 7 + hy] + fresh)
        plane[pl.ds(8, hy, stride=2), :] = even
        last = smooth[8 + hy : 9 + hy] - 0.25 * (
            detail[7 + hy : 8 + hy] + detail[8 + hy : 9 + hy]
        )
        plane[y + 8 : y + 9] = jnp.where(keep_next, last, 0.0)
        after = plane[pl.ds(10, hy, stride=2), :]
        plane[pl.ds(9, hy, stride=2), :] = fresh + 0.5 * (even + after)

    def unlift_detail(k):
        lv = levels[k]
        dx, b1, b2 = lv_refs[k][7], lv_refs[k][9], lv_refs[k][10]
        each(lv.h + 2, lambda i: unlift_y(lv, b1.at[i], b2.at[i], dx.at[i]))

    def unlift_smooth(k, coarse):
        lv = levels[k]
        sx, b0 = lv_refs[k][6], lv_refs[k][8]
        shift = 0 if k + 1 == LEVELS else 1
        each(
            lv.h + 1, lambda i: unlift_y(lv, coarse.at[i + shift], b0.at[i], sx.at[i])
        )

    def unlift_x(k, target, emit=None):
        lv = levels[k]
        sx, dx = lv_refs[k][6], lv_refs[k][7]
        n, h = lv.n, lv.h
        target[1] = sx[0] - 0.25 * (dx[0] + dx[1])

        @pl.when(jnp.logical_not(last_x))
        def _():
            target[n + 1] = sx[h] - 0.25 * (dx[h] + dx[h + 1])

        @pl.when(last_x)
        def _():
            target[n + 1] = jnp.zeros_like(target[n + 1])

        def step(i):
            even = target[2 * i + 1]
            middle = dx[i + 1]
            after = sx[i + 1] - 0.25 * (middle + dx[i + 2])
            target[2 * i + 3] = after
            odd = middle + 0.5 * (even + after)
            target[2 * i + 2] = odd
            if emit is not None:
                emit(2 * i, even)
                emit(2 * i + 1, odd)

        each(h - 1, step)
        even, after, middle = target[n - 1], target[n + 1], dx[h]
        odd = middle + 0.5 * (even + after)
        target[n] = odd
        if emit is not None:
            emit(n - 2, even)
            emit(n - 1, odd)

    mats_s5 = per[LEVELS * width]

    send(0)
    for k in range(LEVELS):
        receive(k)
        fill(k)
        lift_x(k)
        lift_smooth(k)
        if k + 1 < LEVELS:
            send(k + 1)
        lift_detail(k)
        weigh_bands(k)
        unlift_detail(k)
    lv = levels[-1]
    each(lv.h + 1, lambda i: weigh(mats_s5, i, 3 * LEVELS))

    def emit(x, value):
        tile = value[8 : 8 + rows_in].T
        xin[0, pl.ds(x, cells, stride=planes_in), :] = tile[:cells]
        xin[1, pl.ds(x, cells, stride=planes_in), :] = tile[cells:]

    coarse = mats_s5
    for k in reversed(range(LEVELS)):
        unlift_smooth(k, coarse)
        for copy in copies(k):
            copy.wait_send()
        coarse = lv_refs[k][0]
        unlift_x(k, coarse, emit if k == 0 else None)

    stores = [
        pltpu.make_async_copy(
            xin.at[side], out_ref.at[:, side * rows_in : (side + 1) * rows_in], in_sem.at[side]
        )
        for side in range(2)
    ]
    for store in stores:
        store.start()
    for store in stores:
        store.wait()


def per_device(counts, control, band_roots):
    vectors, layers, planes, cols = control.shape
    rows = cols // 2
    levels = levels_of(planes, rows)
    cells = vectors * layers
    x = control.reshape(cells * planes, cols)
    scratch = [
        pltpu.VMEM((2, cells * planes, rows), F32),
        pltpu.VMEM((16, 256, 256), BF16),
        pltpu.SemaphoreType.DMA((2,)),
        pltpu.SemaphoreType.DMA((LEVELS, 12)),
        pltpu.SemaphoreType.DMA((LEVELS, 12)),
    ]
    for lv in levels:
        scratch += [
            pltpu.VMEM((lv.n + 4, lv.r, 128), F32),
            pltpu.VMEM((2, lv.y, 128), F32),
            pltpu.VMEM((2, lv.sent, 128), F32),
            pltpu.VMEM((1, lv.sent, 128), F32),
            pltpu.VMEM((2, lv.got, 128), F32),
            pltpu.VMEM((1, lv.got, 128), F32),
            pltpu.VMEM((lv.h + 1, lv.r, 128), F32),
            pltpu.VMEM((lv.h + 2, lv.r, 128), F32),
            pltpu.VMEM((lv.h + 1, lv.rb, 128), F32),
            pltpu.VMEM((lv.h + 2, lv.rb, 128), F32),
            pltpu.VMEM((lv.h + 2, lv.rb, 128), F32),
        ]
    scratch.append(pltpu.VMEM((levels[-1].h + 1, levels[-1].rb, 128), F32))
    out = pl.pallas_call(
        partial(kernel, levels, counts),
        out_shape=jax.ShapeDtypeStruct((cells * planes, cols), F32),
        in_specs=[
            pl.BlockSpec(memory_space=pl.ANY),
            pl.BlockSpec(memory_space=pltpu.VMEM),
        ],
        out_specs=pl.BlockSpec(memory_space=pl.ANY),
        scratch_shapes=scratch,
        compiler_params=pltpu.CompilerParams(
            collective_id=0, has_side_effects=True, vmem_limit_bytes=48 << 20
        ),
        name="wavelet",
    )(x, band_roots)
    return out.reshape(control.shape)


def solution(mesh):
    counts = (mesh.shape["gx"], mesh.shape["gy"])
    in_specs = (P(None, None, "gx", "gy"), P())
    out_specs = P(None, None, "gx", "gy")
    return jax.shard_map(
        partial(per_device, counts),
        mesh=mesh,
        in_specs=in_specs,
        out_specs=out_specs,
        check_vma=False,
    )
```

```python
from functools import partial

import jax
import jax.numpy as jnp
from jax import lax
from jax.experimental import pallas as pl
from jax.experimental.pallas import tpu as pltpu
from jax.sharding import PartitionSpec as P

LEVELS = 5
F32 = jnp.float32
BF16 = jnp.bfloat16


def round_up(value, step):
    return (value + step - 1) // step * step


class Level:
    def __init__(self, planes, rows):
        self.n = planes
        self.y = rows
        self.h = planes // 2
        self.hy = rows // 2
        self.r = round_up(rows + 16, 16)
        self.rb = round_up(self.hy + 16, 16)
        self.npad = max(planes, 8)
        self.short = planes < 3
        self.sent = self.npad + 16
        self.got = self.npad + 24


def levels_of(planes, rows):
    return [Level(planes >> k, rows >> k) for k in range(LEVELS)]


def each(count, body, unroll_to=4):
    if count <= unroll_to:
        for i in range(count):
            body(i)
    else:

        @pl.loop(0, count)
        def _(i):
            body(i)


def kernel(levels, counts, x_hbm, w_hbm, out_ref, *scratch):
    count_x, count_y = counts
    (xin, w_ref, mats, in_sem, send_sem, recv_sem) = scratch[:6]
    per = scratch[6:]
    width = 11
    lv_refs = [per[k * width : (k + 1) * width] for k in range(LEVELS)]
    gx = lax.axis_index("gx")
    gy = lax.axis_index("gy")
    first_x, last_x = gx == 0, gx == count_x - 1
    planes_in = levels[0].n
    rows_in = levels[0].y
    cells = xin.shape[1] // planes_in

    def at(dx, dy):
        return {
            "gx": lax.rem(gx + dx + count_x, count_x),
            "gy": lax.rem(gy + dy + count_y, count_y),
        }

    friends = [
        (dx, dy) for dx in (-2, -1, 0, 1, 2) for dy in (-1, 0, 1) if (dx, dy) != (0, 0)
    ]
    barrier = pltpu.get_barrier_semaphore()
    for dx, dy in friends:
        pl.semaphore_signal(
            barrier, inc=1, device_id=at(dx, dy), device_id_type=pl.DeviceIdType.MESH
        )

    w_load = pltpu.make_async_copy(w_hbm, w_ref, in_sem.at[2])
    loads = [
        pltpu.make_async_copy(
            x_hbm.at[:, side * rows_in : (side + 1) * rows_in], xin.at[side], in_sem.at[side]
        )
        for side in range(2)
    ]
    for load in loads:
        load.start()
    w_load.start()

    lane = lax.broadcasted_iota(jnp.int32, (1, 128), 1)
    upper = lane >= 64
    keep_next = jnp.logical_or(lane < 64, gy < count_y - 1)
    keep_prev = jnp.logical_or(lane >= 64, gy > 0)

    block_row = lax.broadcasted_iota(jnp.int32, (128, 128), 0) // 32
    block_lane = lax.broadcasted_iota(jnp.int32, (128, 128), 1) // 32
    diagonal = block_row == block_lane

    def build(band):
        small = jnp.concatenate([w_ref[band]] * 4, axis=1)
        tiled = jnp.concatenate([small] * 4, axis=0)
        square = jnp.where(diagonal, tiled, 0.0).T
        high = square.astype(BF16)
        low = (square - high.astype(F32)).astype(BF16)
        mats[band, 0:128, 0:128] = high
        mats[band, 128:256, 0:128] = high
        mats[band, 0:128, 128:256] = low
        mats[band, 128:256, 128:256] = jnp.zeros((128, 128), BF16)

    for load in loads:
        load.wait()

    def take(x):
        low = xin[0, pl.ds(x, cells, stride=planes_in), :]
        high = xin[1, pl.ds(x, cells, stride=planes_in), :]
        tile = jnp.concatenate([low, high], axis=0)
        lv_refs[0][0][x + 1, 8 : 8 + rows_in, :] = tile.T

    each(planes_in, take)

    pl.semaphore_wait(barrier, len(friends))

    def copies(k):
        lv = levels[k]
        a, sp, en, es, rn, rs = lv_refs[k][:6]
        rows = pl.ds(8, lv.y)
        moves = [
            (a.at[1, rows], a.at[lv.n + 1, rows], (-1, 0)),
            (a.at[2, rows] if lv.short else sp.at[0], a.at[lv.n + 2, rows], (-1, 0)),
            (sp.at[1], a.at[0, rows], (1, 0)),
        ]
        if lv.short:
            moves.append((a.at[1, rows], a.at[lv.n + 3, rows], (-2, 0)))
        groups = [
            (pl.ds(0, lv.npad), pl.ds(0, lv.npad), 0),
            (pl.ds(lv.npad, 8), pl.ds(lv.npad, 8), -1),
            (pl.ds(lv.npad + 8, 8), pl.ds(lv.npad + 8, 8), 1),
        ]
        if lv.short:
            groups.append((pl.ds(lv.npad, 8), pl.ds(lv.npad + 16, 8), -2))
        for source, target, dx in groups:
            moves.append((en.at[:, source], rn.at[:, target], (dx, -1)))
            moves.append((es.at[:, source], rs.at[:, target], (dx, 1)))
        ways = {}
        for m, (source, target, way) in enumerate(moves):
            copy = pltpu.make_async_remote_copy(
                src_ref=source,
                dst_ref=target,
                send_sem=send_sem.at[k, m],
                recv_sem=recv_sem.at[k, m],
                device_id=at(*way),
                device_id_type=pl.DeviceIdType.MESH,
            )
            ways.setdefault(way, []).append(copy)
        return ways

    def exists(dx, dy):
        x, y = gx + dx, gy + dy
        inside_x = jnp.logical_and(x >= 0, x < count_x)
        return jnp.logical_and(inside_x, jnp.logical_and(y >= 0, y < count_y))

    def start(ways, wanted):
        for way, group in ways.items():
            if wanted(*way):

                @pl.when(exists(*way))
                def _():
                    for copy in group:
                        copy.start()

    def arrive(ways, wanted):
        for (dx, dy), group in ways.items():
            if wanted(dx, dy):

                @pl.when(exists(-dx, -dy))
                def _():
                    for copy in group:
                        copy.wait_recv()

    def sent(ways):
        for way, group in ways.items():

            @pl.when(exists(*way))
            def _():
                for copy in group:
                    copy.wait_send()

    def send(k):
        lv = levels[k]
        a, sp, en, es = lv_refs[k][:4]
        n, y = lv.n, lv.y
        todo = copies(k)
        rows = pl.ds(8, y)
        if not lv.short:
            sp[0] = a[2, rows] - 0.5 * (a[1, rows] + a[3, rows])
        sp[1] = a[n, rows] - 0.5 * a[n - 1, rows]
        start(todo, lambda dx, dy: dy == 0)
        flat = a.reshape((lv.n + 4) * lv.r, 128)
        line = lambda row: flat[pl.ds(lv.r + row, n, stride=lv.r), :]
        r0 = line(8)
        f_edge, d_edge = r0, line(9) - 0.5 * (r0 + line(10))
        q_edge = line(y + 7) - 0.5 * line(y + 6)
        for ref, kind, edge in ((en, 0, f_edge), (en, 1, d_edge), (es, 0, q_edge)):
            ref[kind, 0:n] = edge
            row = lambda i: ref[kind, i : i + 1]
            ref[kind, lv.npad : lv.npad + 1] = row(0)
            second = row(1) if lv.short else row(1) - 0.5 * (row(0) + row(2))
            ref[kind, lv.npad + 1 : lv.npad + 2] = second
            ref[kind, lv.npad + 8 : lv.npad + 9] = row(n - 1) - 0.5 * row(n - 2)
        start(todo, lambda dx, dy: dy != 0)

    def turn(value):
        return pltpu.roll(value, 64, 1)

    def fill(k):
        lv = levels[k]
        a, sp, en, es, rn, rs = lv_refs[k][:6]
        n, y = lv.n, lv.y
        todo = copies(k)
        flat = a.reshape((lv.n + 4) * lv.r, 128)

        def place(plane, count, f_here, d_here, q_here, slot):
            slot = pl.ds(slot, count)

            def put(row, value):
                flat[pl.ds(plane * lv.r + row, count, stride=lv.r), :] = value

            f_all = turn(jnp.where(upper, f_here, rn[0, slot]))
            d_all = turn(jnp.where(upper, d_here, rn[1, slot]))
            put(y + 8, jnp.where(keep_next, f_all, 0.0))
            put(y + 9, jnp.where(keep_next, d_all, 0.0))
            put(7, turn(jnp.where(upper, rs[0, slot], q_here)))

        arrive(todo, lambda dx, dy: dx == 0)
        place(1, n, en[0, 0:n], en[1, 0:n], es[0, 0:n], 0)
        arrive(todo, lambda dx, dy: dx != 0)
        halo = [(n + 1, lv.npad), (n + 2, lv.npad + 1), (0, lv.npad + 8)]
        if lv.short:
            halo.append((n + 3, lv.npad + 16))
        for plane, slot in halo:
            r0, r1, r2 = a[plane, 8:9], a[plane, 9:10], a[plane, 10:11]
            before, end = a[plane, y + 6 : y + 7], a[plane, y + 7 : y + 8]
            place(plane, 1, r0, r1 - 0.5 * (r0 + r2), end - 0.5 * before, slot)
        if lv.short:

            @pl.when(gx == count_x - 2)
            def _():
                a[n + 3] = jnp.zeros_like(a[n + 3])

            a[n + 2] = a[n + 2] - 0.5 * (a[n + 1] + a[n + 3])

        @pl.when(last_x)
        def _():
            a[n + 1] = jnp.zeros_like(a[n + 1])
            a[n + 2] = jnp.zeros_like(a[n + 2])

        @pl.when(first_x)
        def _():
            a[0] = 0.5 * a[1]

    def lift_x(k):
        lv = levels[k]
        a, sx, dx = lv_refs[k][0], lv_refs[k][6], lv_refs[k][7]
        n, h = lv.n, lv.h
        dx[0] = a[0] - 0.5 * a[1]

        def step(i):
            even = a[2 * i + 1]
            detail = a[2 * i + 2] - 0.5 * (even + a[2 * i + 3])
            dx[i + 1] = detail
            sx[i] = even + 0.25 * (dx[i] + detail)

        each(h, step)
        dx[h + 1] = a[n + 2]
        sx[h] = a[n + 1] + 0.25 * (dx[h] + dx[h + 1])

    def lift_y(lv, plane, smooth, detail):
        hy, y = lv.hy, lv.y
        even = plane[pl.ds(8, hy, stride=2), :]
        odd = plane[pl.ds(9, hy, stride=2), :]
        after = plane[pl.ds(10, hy, stride=2), :]
        fresh = odd - 0.5 * (even + after)
        detail[8 : 8 + hy] = fresh
        detail[7:8] = jnp.where(keep_prev, plane[7:8] - 0.5 * plane[8:9], 0.0)
        detail[8 + hy : 9 + hy] = plane[y + 9 : y + 10]
        if smooth is None:
            return
        smooth[8 : 8 + hy] = even + 0.25 * (detail[7 : 7 + hy] + fresh)
        smooth[8 + hy : 9 + hy] = plane[y + 8 : y + 9] + 0.25 * (
            detail[7 + hy : 8 + hy] + detail[8 + hy : 9 + hy]
        )

    def lift_smooth(k):
        lv = levels[k]
        sx, b0 = lv_refs[k][6], lv_refs[k][8]
        coarse = lv_refs[k + 1][0] if k + 1 < LEVELS else None
        if coarse is None:
            target = mats_s5

            def step(i):
                lift_y(lv, sx.at[i], target.at[i], b0.at[i])

            each(lv.h + 1, step)
        else:

            def step(i):
                lift_y(lv, sx.at[i], coarse.at[i + 1], b0.at[i])

            each(lv.h, step)
            lift_y(lv, sx.at[lv.h], None, b0.at[lv.h])

    def lift_detail(k):
        lv = levels[k]
        dx, b1, b2 = lv_refs[k][7], lv_refs[k][9], lv_refs[k][10]

        def step(i):
            lift_y(lv, dx.at[i], b1.at[i], b2.at[i])

        each(lv.h + 2, step)

    def weigh(ref, band, most=512):
        planes, rows, _ = ref.shape
        chunk = planes
        while chunk * rows > most and chunk % 3 == 0:
            chunk //= 3

        def step(i):
            value = ref[pl.ds(i * chunk, chunk)].reshape(chunk * rows, 128)
            high = value.astype(BF16)
            low = (value - high.astype(F32)).astype(BF16)
            both = jnp.concatenate([high, low], axis=1)
            product = jnp.dot(both, mats[band], preferred_element_type=F32)
            total = product[:, :128] + product[:, 128:]
            ref[pl.ds(i * chunk, chunk)] = total.reshape(chunk, rows, 128)

        each(planes // chunk, step, 1)

    def weigh_bands(k):
        for offset in range(3):
            weigh(lv_refs[k][8 + offset], 3 * k + offset)

    def unlift_y(lv, smooth, detail, plane):
        hy, y = lv.hy, lv.y
        fresh = detail[8 : 8 + hy]
        even = smooth[8 : 8 + hy] - 0.25 * (detail[7 : 7 + hy] + fresh)
        plane[pl.ds(8, hy, stride=2), :] = even
        last = smooth[8 + hy : 9 + hy] - 0.25 * (
            detail[7 + hy : 8 + hy] + detail[8 + hy : 9 + hy]
        )
        plane[y + 8 : y + 9] = jnp.where(keep_next, last, 0.0)
        after = plane[pl.ds(10, hy, stride=2), :]
        plane[pl.ds(9, hy, stride=2), :] = fresh + 0.5 * (even + after)

    def unlift_detail(k):
        lv = levels[k]
        dx, b1, b2 = lv_refs[k][7], lv_refs[k][9], lv_refs[k][10]
        each(lv.h + 2, lambda i: unlift_y(lv, b1.at[i], b2.at[i], dx.at[i]))

    def unlift_smooth(k, coarse):
        lv = levels[k]
        sx, b0 = lv_refs[k][6], lv_refs[k][8]
        shift = 0 if k + 1 == LEVELS else 1
        each(
            lv.h + 1, lambda i: unlift_y(lv, coarse.at[i + shift], b0.at[i], sx.at[i])
        )

    def unlift_x(k, target, emit=None):
        lv = levels[k]
        sx, dx = lv_refs[k][6], lv_refs[k][7]
        n, h = lv.n, lv.h
        target[1] = sx[0] - 0.25 * (dx[0] + dx[1])

        @pl.when(jnp.logical_not(last_x))
        def _():
            target[n + 1] = sx[h] - 0.25 * (dx[h] + dx[h + 1])

        @pl.when(last_x)
        def _():
            target[n + 1] = jnp.zeros_like(target[n + 1])

        def step(i):
            even = target[2 * i + 1]
            middle = dx[i + 1]
            after = sx[i + 1] - 0.25 * (middle + dx[i + 2])
            target[2 * i + 3] = after
            odd = middle + 0.5 * (even + after)
            target[2 * i + 2] = odd
            if emit is not None:
                emit(2 * i, even)
                emit(2 * i + 1, odd)

        each(h - 1, step)
        even, after, middle = target[n - 1], target[n + 1], dx[h]
        odd = middle + 0.5 * (even + after)
        target[n] = odd
        if emit is not None:
            emit(n - 2, even)
            emit(n - 1, odd)

    mats_s5 = per[LEVELS * width]

    send(0)
    w_load.wait()
    each(16, build)
    for k in range(LEVELS):
        fill(k)
        lift_x(k)
        lift_smooth(k)
        if k + 1 < LEVELS:
            send(k + 1)
        lift_detail(k)
        weigh_bands(k)
        unlift_detail(k)
    weigh(mats_s5, 3 * LEVELS)

    def emit(x, value):
        tile = value[8 : 8 + rows_in].T
        base = (x // 8) * 16 + lax.rem(x, 8)
        out_ref[pl.ds(base, cells, stride=2 * planes_in), :] = tile[:cells]
        out_ref[pl.ds(base + 8, cells, stride=2 * planes_in), :] = tile[cells:]

    coarse = mats_s5
    for k in reversed(range(LEVELS)):
        unlift_smooth(k, coarse)
        sent(copies(k))
        coarse = lv_refs[k][0]
        unlift_x(k, coarse, emit if k == 0 else None)


def per_device(counts, control, band_roots):
    vectors, layers, planes, cols = control.shape
    rows = cols // 2
    levels = levels_of(planes, rows)
    cells = vectors * layers
    x = control.reshape(cells * planes, cols)
    scratch = [
        pltpu.VMEM((2, cells * planes, rows), F32),
        pltpu.VMEM(band_roots.shape, F32),
        pltpu.VMEM((16, 256, 256), BF16),
        pltpu.SemaphoreType.DMA((3,)),
        pltpu.SemaphoreType.DMA((LEVELS, 12)),
        pltpu.SemaphoreType.DMA((LEVELS, 12)),
    ]
    for lv in levels:
        scratch += [
            pltpu.VMEM((lv.n + 4, lv.r, 128), F32),
            pltpu.VMEM((2, lv.y, 128), F32),
            pltpu.VMEM((2, lv.sent, 128), F32),
            pltpu.VMEM((1, lv.sent, 128), F32),
            pltpu.VMEM((2, lv.got, 128), F32),
            pltpu.VMEM((1, lv.got, 128), F32),
            pltpu.VMEM((lv.h + 1, lv.r, 128), F32),
            pltpu.VMEM((lv.h + 2, lv.r, 128), F32),
            pltpu.VMEM((lv.h + 2, lv.rb, 128), F32),
            pltpu.VMEM((lv.h + 2, lv.rb, 128), F32),
            pltpu.VMEM((lv.h + 2, lv.rb, 128), F32),
        ]
    scratch.append(pltpu.VMEM((levels[-1].h + 1, levels[-1].rb, 128), F32))
    out = pl.pallas_call(
        partial(kernel, levels, counts),
        out_shape=jax.ShapeDtypeStruct((cells * planes * 2, rows), F32),
        in_specs=[
            pl.BlockSpec(memory_space=pltpu.HBM),
            pl.BlockSpec(memory_space=pltpu.HBM),
        ],
        out_specs=pl.BlockSpec(memory_space=pltpu.VMEM),
        scratch_shapes=scratch,
        compiler_params=pltpu.CompilerParams(
            collective_id=0, has_side_effects=True, vmem_limit_bytes=54000000
        ),
        name="wavelet",
    )(x, band_roots)
    out = out.reshape(cells * planes // 8, 2, 8, rows).transpose(0, 2, 1, 3)
    return out.reshape(control.shape)


def solution(mesh):
    counts = (mesh.shape["gx"], mesh.shape["gy"])
    in_specs = (P(None, None, "gx", "gy"), P())
    out_specs = P(None, None, "gx", "gy")
    return jax.shard_map(
        partial(per_device, counts),
        mesh=mesh,
        in_specs=in_specs,
        out_specs=out_specs,
        check_vma=False,
    )
```

```python
from functools import partial

import jax
import jax.numpy as jnp
from jax import lax
from jax.experimental import pallas as pl
from jax.experimental.pallas import tpu as pltpu
from jax.sharding import PartitionSpec as P

LEVELS = 5
F32 = jnp.float32
BF16 = jnp.bfloat16


def round_up(value, step):
    return (value + step - 1) // step * step


class Level:
    def __init__(self, planes, rows, first, last):
        self.n = planes
        self.y = rows
        self.h = planes // 2
        self.hy = rows // 2
        self.first = first
        self.last = last
        self.r = round_up(rows + 10, 8)
        self.rb = round_up(self.hy + 10, 16)
        self.rs = round_up(self.hy + 3, 8)
        self.hp = round_up(self.h + 3, 8)
        self.bands = 4 if last else 3
        self.kinds = ["sd", "ds", "dd", "ss"][: self.bands]
        self.reach = 2 if self.h == 1 else 1

    def x_strip(self, kind, hop):
        low = -1 if kind == "d" else 0
        high = self.h + (1 if kind == "s" else 0)
        begin = max(low, -1 - hop * self.h)
        end = min(self.h, high - hop * self.h)
        return begin + hop * self.h, begin, end - begin + 1

    def y_rows(self, kind, hop):
        if hop < 0:
            return -1, self.hy - 1
        return (self.hy - 1, -1) if kind == "d" else (self.hy, 0)


def levels_of(planes, rows):
    return [
        Level(planes >> k, rows >> k, k == 0, k == LEVELS - 1) for k in range(LEVELS)
    ]


def each(count, body, unroll_to=4):
    if count <= unroll_to:
        for i in range(count):
            body(i)
    else:

        @pl.loop(0, count)
        def _(i):
            body(i)


NAMES = (
    "a",
    "sx",
    "dx",
    "b0",
    "b1",
    "b2",
    "b3",
    "yl",
    "yr",
    "ryl",
    "ryr",
    "cs",
    "cr",
    "xsl",
    "xsr",
    "xrl",
    "xrr",
    "xfs",
    "xfr",
)


def kernel(levels, counts, x_hbm, w_hbm, out_ref, *scratch):
    count_x, count_y = counts
    (xin, w_ref, mats, temp, in_sem, send_sem, recv_sem) = scratch[:7]
    per = scratch[7:]
    refs = [
        dict(zip(NAMES, per[k * len(NAMES) : (k + 1) * len(NAMES)])) for k in range(LEVELS)
    ]
    gx = lax.axis_index("gx")
    gy = lax.axis_index("gy")
    first_x, last_x = gx == 0, gx == count_x - 1
    planes_in = levels[0].n
    rows_in = levels[0].y
    cells = xin.shape[1] // planes_in

    def at(dx, dy):
        return {
            "gx": lax.rem(gx + dx + count_x, count_x),
            "gy": lax.rem(gy + dy + count_y, count_y),
        }

    friends = [
        (dx, dy) for dx in (-2, -1, 0, 1, 2) for dy in (-1, 0, 1) if (dx, dy) != (0, 0)
    ]
    barrier = pltpu.get_barrier_semaphore()
    for dx, dy in friends:
        pl.semaphore_signal(
            barrier, inc=1, device_id=at(dx, dy), device_id_type=pl.DeviceIdType.MESH
        )
    w_load = pltpu.make_async_copy(w_hbm, w_ref, in_sem.at[2])
    loads = [
        pltpu.make_async_copy(
            x_hbm.at[:, side * rows_in : (side + 1) * rows_in], xin.at[side], in_sem.at[side]
        )
        for side in range(2)
    ]
    for load in loads:
        load.start()
    w_load.start()

    lane = lax.broadcasted_iota(jnp.int32, (1, 128), 1)
    upper = lane >= 64
    keep_next = jnp.logical_or(lane < 64, gy < count_y - 1)
    keep_prev = jnp.logical_or(lane >= 64, gy > 0)
    not_first = jnp.where(first_x, 0.0, 1.0).astype(F32)

    block_row = lax.broadcasted_iota(jnp.int32, (128, 128), 0) // 32
    block_lane = lax.broadcasted_iota(jnp.int32, (128, 128), 1) // 32
    diagonal = block_row == block_lane

    def build(band):
        small = jnp.concatenate([w_ref[band]] * 4, axis=1)
        tiled = jnp.concatenate([small] * 4, axis=0)
        square = jnp.where(diagonal, tiled, 0.0).T
        high = square.astype(BF16)
        low = (square - high.astype(F32)).astype(BF16)
        mats[band, 0:128, 0:128] = high
        mats[band, 128:256, 0:128] = high
        mats[band, 0:128, 128:256] = low
        mats[band, 128:256, 128:256] = jnp.zeros((128, 128), BF16)

    def rows_of(ref, plane, count, row):
        planes, height, _ = ref.shape
        flat = ref.reshape(planes * height, 128)
        return flat, pl.ds(plane * height + row, count, stride=height)

    def gather(ref, plane, count, row):
        flat, where = rows_of(ref, plane, count, row)
        return flat[where, :]

    def scatter(ref, plane, count, row, value):
        flat, where = rows_of(ref, plane, count, row)
        flat[where, :] = value

    top = refs[0]["a"]
    for plane in (0, planes_in + 1, planes_in + 2):
        top[plane] = jnp.zeros(top.shape[1:], F32)
    for row in (7, rows_in + 8, rows_in + 9):
        scatter(top, 1, planes_in, row, jnp.zeros((planes_in, 128), F32))

    edge_right, edge_left = refs[0]["xrr"], refs[0]["xrl"]
    for edge in (edge_right, edge_left):
        for plane in range(edge.shape[0]):
            edge[plane, 0:8] = jnp.zeros((8, 128), F32)
            edge[plane, rows_in + 8 : rows_in + 16] = jnp.zeros((8, 128), F32)

    for load in loads:
        load.wait()

    def take(x):
        low = xin[0, pl.ds(x, cells, stride=planes_in), :]
        high = xin[1, pl.ds(x, cells, stride=planes_in), :]
        tile = jnp.concatenate([low, high], axis=0)
        top[x + 1, 8 : 8 + rows_in, :] = tile.T

    def copies(k):
        lv, r = levels[k], refs[k]
        landing = pl.ds(8, rows_in) if lv.first else pl.ds(0, lv.rs)
        moves = [
            (r["xsl"], r["xrr"].at[:, landing], (-1, 0)),
            (r["xsr"], r["xrl"].at[:, landing], (1, 0)),
        ]
        if lv.reach == 2:
            moves.append((r["xfs"].at[0], r["xfr"].at[0], (-2, 0)))
            moves.append((r["xfs"].at[1], r["xfr"].at[1], (2, 0)))
        moves.append((r["yl"], r["ryl"], (0, -1)))
        moves.append((r["yr"], r["ryr"], (0, 1)))
        for i, (hop, way) in enumerate(corners(lv)):
            moves.append((r["cs"].at[i], r["cr"].at[i], (hop, way)))
        ways = {}
        for m, (source, target, way) in enumerate(moves):
            copy = pltpu.make_async_remote_copy(
                src_ref=source,
                dst_ref=target,
                send_sem=send_sem.at[k, m],
                recv_sem=recv_sem.at[k, m],
                device_id=at(*way),
                device_id_type=pl.DeviceIdType.MESH,
            )
            ways.setdefault(way, []).append(copy)
        return ways

    def exists(dx, dy):
        x, y = gx + dx, gy + dy
        inside_x = jnp.logical_and(x >= 0, x < count_x)
        return jnp.logical_and(inside_x, jnp.logical_and(y >= 0, y < count_y))

    def start(ways, wanted):
        for way, group in ways.items():
            if wanted(*way):

                @pl.when(exists(*way))
                def _():
                    for copy in group:
                        copy.start()

    def arrive(ways):
        for (dx, dy), group in ways.items():

            @pl.when(exists(-dx, -dy))
            def _():
                for copy in group:
                    copy.wait_recv()

    def sent(ways):
        for way, group in ways.items():

            @pl.when(exists(*way))
            def _():
                for copy in group:
                    copy.wait_send()

    def send_first():
        n, rows = planes_in, pl.ds(8, rows_in)
        low, high = refs[0]["xsl"], refs[0]["xsr"]
        low[0] = top[1, rows]
        low[1] = top[2, rows] - 0.5 * (top[1, rows] + top[3, rows])
        high[0] = top[n, rows] - 0.5 * top[n - 1, rows]
        start(copies(0), lambda dx, dy: dy == 0)

    def send(k):
        lv, r = levels[k], refs[k]
        todo = copies(k)
        if not lv.first:
            whole, part = slice(7, lv.hy + 10), slice(0, lv.hy + 3)
            for name, low, single in (("xsl", 0, 1), ("xsr", lv.h, lv.h + 1)):
                for i in range(2):
                    r[name][i, part] = r["b1"][low + i, whole]
                    r[name][2 + i, part] = r["b2"][low + i, whole]
                r[name][4, part] = r["b0"][single, whole]
                if lv.last:
                    r[name][5, part] = r["b3"][single, whole]
            if lv.reach == 2:
                for place, plane in ((0, 0), (1, lv.h + 1)):
                    for t in (1, 2):
                        r["xfs"][place, t - 1, part] = r[f"b{t}"][plane, whole]
            start(todo, lambda dx, dy: dy == 0)
        planes = lv.h + 3
        for t, kind in enumerate(lv.kinds):
            for name, hop in (("yl", -1), ("yr", 1)):
                source, _ = lv.y_rows(kind[1], hop)
                for i in range(2):
                    count = planes if kind[0] == "s" else planes - 1
                    value = gather(r[f"b{t}"], 0, count, 8 + source + i)
                    r[name][2 * t + i, 0:count] = value
        for c, (hop, way) in enumerate(corners(lv)):
            strips = r["yl"] if way < 0 else r["yr"]
            for t, kind in enumerate(lv.kinds):
                source, _, count = lv.x_strip(kind[0], hop)
                planes = slice(source + 1, source + 1 + count)
                one, two = strips[2 * t, planes], strips[2 * t + 1, planes]
                if way < 0:
                    both = jnp.where(upper, pltpu.roll(two, 64, 1), one)
                else:
                    both = jnp.where(upper, two, pltpu.roll(one, 64, 1))
                r["cs"][c, 2 * t : 2 * t + count] = both
        start(todo, lambda dx, dy: dy != 0)

    def collect(k):
        lv, r = levels[k], refs[k]
        h = lv.h
        todo = copies(k)
        arrive(todo)
        whole, part = slice(7, lv.hy + 10), slice(0, lv.hy + 3)

        def add(t, position, value):
            r[f"b{t}"][position + 1, whole] = r[f"b{t}"][position + 1, whole] + value

        if lv.first:
            smooth_of = lambda i: temp[2 * i, whole]
            detail_of = lambda i: temp[2 * i + 1, whole]

            @pl.when(gx > 0)
            def _():
                lift_y(lv, edge_left.at[0], temp.at[0], temp.at[1], False)
                add(1, -1, smooth_of(0))
                add(2, -1, detail_of(0))
                add(0, 0, 0.25 * detail_of(0))

            @pl.when(gx < count_x - 1)
            def _():
                for i in range(2):
                    out = 2 + 2 * i
                    lift_y(lv, edge_right.at[i], temp.at[out], temp.at[out + 1], False)
                add(1, h - 1, -0.5 * smooth_of(1))
                add(2, h - 1, -0.5 * detail_of(1))
                add(1, h, smooth_of(2))
                add(2, h, detail_of(2))
                add(0, h - 1, -0.125 * detail_of(1))
                add(0, h, 0.875 * detail_of(1) + 0.25 * detail_of(2))

        else:
            smooth = [(0, 4, 2)] if lv.bands == 3 else [(0, 4, 2), (3, 5, 0)]
            from_left = lambda i: r["xrl"][i, part]
            from_right = lambda i: r["xrr"][i, part]

            @pl.when(gx > 0)
            def _():
                for t in (1, 2):
                    add(t, -1, from_left(2 * t - 2))
                    add(t, 0, from_left(2 * t - 1))
                for t, slot, d in smooth:
                    add(t, 0, from_left(slot))
                    add(t, 1, 0.25 * from_left(d + 1))

            @pl.when(gx < count_x - 1)
            def _():
                for t in (1, 2):
                    add(t, h - 1, from_right(2 * t - 2))
                    add(t, h, from_right(2 * t - 1))
                for t, slot, d in smooth:
                    add(t, h - 1, 0.25 * from_right(d))
                    add(t, h, from_right(slot))

            if lv.reach == 2:
                far = lambda side, d: r["xfr"][side, d, part]

                @pl.when(gx > 1)
                def _():
                    for t in (1, 2):
                        add(t, -1, far(1, t - 1))
                    for t, _, d in smooth:
                        add(t, 0, 0.25 * far(1, d // 2))

                @pl.when(gx < count_x - 2)
                def _():
                    for t in (1, 2):
                        add(t, h, far(0, t - 1))
                    for t, _, d in smooth:
                        add(t, h, 0.25 * far(0, d // 2))

        for c, (hop, way) in enumerate(corners(lv)):
            strips = r["ryl"] if way < 0 else r["ryr"]

            @pl.when(exists(-hop, -way))
            def _():
                for t, kind in enumerate(lv.kinds):
                    _, target, count = lv.x_strip(kind[0], hop)
                    packed = r["cr"][c, 2 * t : 2 * t + count]
                    other = pltpu.roll(packed, 64, 1)
                    planes = slice(target + 1, target + 1 + count)
                    for i in range(2):
                        value = packed if (way < 0) == (i == 0) else other
                        strips[2 * t + i, planes] = strips[2 * t + i, planes] + value

        planes = h + 2
        for t, kind in enumerate(lv.kinds):
            band = r[f"b{t}"]
            todo_rows = []
            for i in range(2):
                source, target = lv.y_rows(kind[1], -1)
                here = gather(band, 0, planes, 8 + source + i)
                there = r["ryl"][2 * t + i, 0:planes]
                moved = pltpu.roll(jnp.where(upper, here, there), 64, 1)
                todo_rows.append((target + i, jnp.where(keep_next, moved, 0.0)))
                source, target = lv.y_rows(kind[1], 1)
                here = gather(band, 0, planes, 8 + source + i)
                there = r["ryr"][2 * t + i, 0:planes]
                moved = pltpu.roll(jnp.where(upper, there, here), 64, 1)
                todo_rows.append((target + i, jnp.where(keep_prev, moved, 0.0)))
            for row, value in todo_rows:
                mine = gather(band, 0, planes, 8 + row)
                scatter(band, 0, planes, 8 + row, mine + value)

    def lift_x(k):
        lv = levels[k]
        a, sx, dx = (refs[k][name] for name in ("a", "sx", "dx"))
        n, h = lv.n, lv.h
        low = not_first * (a[0] - 0.5 * a[1])
        dx[0] = low
        sx[0] = 0.25 * low

        def step(i):
            even = a[2 * i + 1]
            detail = a[2 * i + 2] - 0.5 * (even + a[2 * i + 3])
            dx[i + 1] = detail
            sx[i + 1] = even + 0.25 * (dx[i] + detail)

        each(h, step)
        high = a[n + 2] - 0.5 * a[n + 1]
        dx[h + 1] = high
        sx[h + 1] = a[n + 1] + 0.25 * (dx[h] + high)
        sx[h + 2] = 0.25 * high

    def lift_y(lv, plane, smooth, detail, mask):
        hy, y = lv.hy, lv.y
        even = plane[pl.ds(8, hy, stride=2), :]
        odd = plane[pl.ds(9, hy, stride=2), :]
        after = plane[pl.ds(10, hy, stride=2), :]
        fresh = odd - 0.5 * (even + after)
        detail[8 : 8 + hy] = fresh
        low = jnp.where(keep_prev, plane[7:8] - 0.5 * plane[8:9], 0.0)
        next_even = plane[y + 8 : y + 9]
        high = plane[y + 9 : y + 10] - 0.5 * next_even
        detail[7:8] = low
        detail[8 + hy : 9 + hy] = high
        smooth[8 : 8 + hy] = even + 0.25 * (detail[7 : 7 + hy] + fresh)
        smooth[7:8] = 0.25 * low
        end = next_even + 0.25 * (detail[7 + hy : 8 + hy] + high)
        end_next = 0.25 * high
        if mask:
            end = jnp.where(keep_next, end, 0.0)
            end_next = jnp.where(keep_next, end_next, 0.0)
        smooth[8 + hy : 9 + hy] = end
        smooth[9 + hy : 10 + hy] = end_next

    def lift_smooth(k):
        lv, r = levels[k], refs[k]
        coarse = r["b3"] if lv.last else refs[k + 1]["a"]
        each(
            lv.h + 3,
            lambda i: lift_y(lv, r["sx"].at[i], coarse.at[i], r["b0"].at[i], not lv.last),
        )
        if not lv.last:

            @pl.when(last_x)
            def _():
                coarse[lv.h + 1] = jnp.zeros_like(coarse[lv.h + 1])
                coarse[lv.h + 2] = jnp.zeros_like(coarse[lv.h + 2])

    def lift_detail(k):
        lv, r = levels[k], refs[k]
        each(
            lv.h + 2,
            lambda i: lift_y(lv, r["dx"].at[i], r["b1"].at[i], r["b2"].at[i], False),
        )

    def weigh(ref, band, begin, planes, most=512):
        rows = ref.shape[1]
        chunk = planes
        while chunk * rows > most and chunk % 3 == 0:
            chunk //= 3

        def step(i):
            part = pl.ds(begin + i * chunk, chunk)
            value = ref[part].reshape(chunk * rows, 128)
            high = value.astype(BF16)
            low = (value - high.astype(F32)).astype(BF16)
            both = jnp.concatenate([high, low], axis=1)
            product = jnp.dot(both, mats[band], preferred_element_type=F32)
            total = product[:, :128] + product[:, 128:]
            ref[part] = total.reshape(chunk, rows, 128)

        each(planes // chunk, step, 1)

    def weigh_bands(k):
        lv, r = levels[k], refs[k]
        for t in range(lv.bands):
            weigh(r[f"b{t}"], 3 * k + t, 0, lv.h + 2)

    def unlift_y(lv, smooth, detail, plane):
        hy, y = lv.hy, lv.y
        fresh = detail[8 : 8 + hy]
        even = smooth[8 : 8 + hy] - 0.25 * (detail[7 : 7 + hy] + fresh)
        plane[pl.ds(8, hy, stride=2), :] = even
        last = smooth[8 + hy : 9 + hy] - 0.25 * (
            detail[7 + hy : 8 + hy] + detail[8 + hy : 9 + hy]
        )
        plane[y + 8 : y + 9] = jnp.where(keep_next, last, 0.0)
        after = plane[pl.ds(10, hy, stride=2), :]
        plane[pl.ds(9, hy, stride=2), :] = fresh + 0.5 * (even + after)

    def unlift_detail(k):
        lv, r = levels[k], refs[k]
        each(lv.h + 2, lambda i: unlift_y(lv, r["b1"].at[i], r["b2"].at[i], r["dx"].at[i]))

    def unlift_smooth(k, coarse):
        lv, r = levels[k], refs[k]
        each(
            lv.h + 1,
            lambda i: unlift_y(lv, coarse.at[i + 1], r["b0"].at[i + 1], r["sx"].at[i + 1]),
        )

    def unlift_x(k, target, emit=None):
        lv = levels[k]
        sx, dx = refs[k]["sx"], refs[k]["dx"]
        n, h = lv.n, lv.h
        target[1] = sx[1] - 0.25 * (dx[0] + dx[1])

        @pl.when(jnp.logical_not(last_x))
        def _():
            target[n + 1] = sx[h + 1] - 0.25 * (dx[h] + dx[h + 1])

        @pl.when(last_x)
        def _():
            target[n + 1] = jnp.zeros_like(target[n + 1])

        def step(i):
            even = target[2 * i + 1]
            middle = dx[i + 1]
            after = sx[i + 2] - 0.25 * (middle + dx[i + 2])
            target[2 * i + 3] = after
            odd = middle + 0.5 * (even + after)
            target[2 * i + 2] = odd
            if emit is not None:
                emit(2 * i, even)
                emit(2 * i + 1, odd)

        each(h - 1, step)
        even, after, middle = target[n - 1], target[n + 1], dx[h]
        odd = middle + 0.5 * (even + after)
        target[n] = odd
        if emit is not None:
            emit(n - 2, even)
            emit(n - 1, odd)

    edge_planes = (0, 1, 2, planes_in - 2, planes_in - 1)
    for x in edge_planes:
        take(x)
    pl.semaphore_wait(barrier, len(friends))
    send_first()

    @pl.loop(0, (planes_in - len(edge_planes)) // 3)
    def _(i):
        for j in range(3):
            take(3 + 3 * i + j)

    for k in range(LEVELS):
        lift_x(k)
        lift_smooth(k)
        lift_detail(k)
        send(k)
    w_load.wait()
    each(16, build)
    for k in range(LEVELS):
        collect(k)
        weigh_bands(k)
        unlift_detail(k)

    def emit(x, value):
        tile = value[8 : 8 + rows_in].T
        base = (x // 8) * 16 + lax.rem(x, 8)
        out_ref[pl.ds(base, cells, stride=2 * planes_in), :] = tile[:cells]
        out_ref[pl.ds(base + 8, cells, stride=2 * planes_in), :] = tile[cells:]

    coarse = refs[LEVELS - 1]["b3"]
    for k in reversed(range(LEVELS)):
        unlift_smooth(k, coarse)
        coarse = refs[k]["a"]
        unlift_x(k, coarse, emit if k == 0 else None)
    for k in range(LEVELS):
        sent(copies(k))


def corners(lv):
    hops = [-1, 1] + ([-2, 2] if lv.reach == 2 else [])
    return [(hop, way) for way in (-1, 1) for hop in hops]


def per_device(counts, control, band_roots):
    vectors, layers, planes, cols = control.shape
    rows = cols // 2
    levels = levels_of(planes, rows)
    cells = vectors * layers
    x = control.reshape(cells * planes, cols)
    scratch = [
        pltpu.VMEM((2, cells * planes, rows), F32),
        pltpu.VMEM(band_roots.shape, F32),
        pltpu.VMEM((16, 256, 256), BF16),
        pltpu.VMEM((6, levels[0].rb, 128), F32),
        pltpu.SemaphoreType.DMA((3,)),
        pltpu.SemaphoreType.DMA((LEVELS, 24)),
        pltpu.SemaphoreType.DMA((LEVELS, 24)),
    ]
    for lv in levels:
        t, h = lv.bands, lv.h
        shapes = dict(
            a=(lv.n + 3, lv.r),
            sx=(h + 3, lv.r),
            dx=(h + 2, lv.r),
            b0=(h + 3, lv.rb),
            b1=(h + 2, lv.rb),
            b2=(h + 2, lv.rb),
            b3=(h + 3, lv.rb),
            yl=(2 * t, lv.hp),
            yr=(2 * t, lv.hp),
            ryl=(2 * t, lv.hp),
            ryr=(2 * t, lv.hp),
            cs=(len(corners(lv)), 8),
            cr=(len(corners(lv)), 8),
            xsl=(2, lv.y) if lv.first else (t + 2, lv.rs),
            xsr=(1, lv.y) if lv.first else (t + 2, lv.rs),
            xrl=(1, lv.y + 16) if lv.first else (t + 2, lv.rs),
            xrr=(2, lv.y + 16) if lv.first else (t + 2, lv.rs),
            xfs=(2, 2, lv.rs),
            xfr=(2, 2, lv.rs),
        )
        for name in NAMES:
            used = {"b3": lv.last, "xfs": lv.last, "xfr": lv.last}.get(name, True)
            scratch.append(pltpu.VMEM((shapes[name] if used else (8,)) + (128,), F32))
    out = pl.pallas_call(
        partial(kernel, levels, counts),
        out_shape=jax.ShapeDtypeStruct((cells * planes * 2, rows), F32),
        in_specs=[
            pl.BlockSpec(memory_space=pltpu.HBM),
            pl.BlockSpec(memory_space=pltpu.HBM),
        ],
        out_specs=pl.BlockSpec(memory_space=pltpu.VMEM),
        scratch_shapes=scratch,
        compiler_params=pltpu.CompilerParams(
            collective_id=0, has_side_effects=True, vmem_limit_bytes=54000000
        ),
        name="wavelet",
    )(x, band_roots)
    out = out.reshape(cells * planes // 8, 2, 8, rows).transpose(0, 2, 1, 3)
    return out.reshape(control.shape)


def solution(mesh):
    counts = (mesh.shape["gx"], mesh.shape["gy"])
    in_specs = (P(None, None, "gx", "gy"), P())
    out_specs = P(None, None, "gx", "gy")
    return jax.shard_map(
        partial(per_device, counts),
        mesh=mesh,
        in_specs=in_specs,
        out_specs=out_specs,
        check_vma=False,
    )
```

```python
from functools import partial

import jax
import jax.numpy as jnp
from jax import lax
from jax.experimental import pallas as pl
from jax.experimental.pallas import tpu as pltpu
from jax.sharding import PartitionSpec as P

LEVELS = 5
F32 = jnp.float32
BF16 = jnp.bfloat16


def round_up(value, step):
    return (value + step - 1) // step * step


class Level:
    def __init__(self, planes, rows, first, last):
        self.n = planes
        self.y = rows
        self.h = planes // 2
        self.hy = rows // 2
        self.first = first
        self.last = last
        self.r = round_up(rows + 10, 8)
        self.rb = round_up(self.hy + 10, 16)
        self.rs = round_up(self.hy + 3, 8)
        self.hp = round_up(self.h + 3, 8)
        self.bands = 4 if last else 3
        self.kinds = ["sd", "ds", "dd", "ss"][: self.bands]
        self.reach = 2 if self.h == 1 else 1

    def x_strip(self, kind, hop):
        low = -1 if kind == "d" else 0
        high = self.h + (1 if kind == "s" else 0)
        begin = max(low, -1 - hop * self.h)
        end = min(self.h, high - hop * self.h)
        return begin + hop * self.h, begin, end - begin + 1

    def y_rows(self, kind, hop):
        if hop < 0:
            return -1, self.hy - 1
        return (self.hy - 1, -1) if kind == "d" else (self.hy, 0)


def levels_of(planes, rows):
    return [
        Level(planes >> k, rows >> k, k == 0, k == LEVELS - 1) for k in range(LEVELS)
    ]


def each(count, body, unroll_to=4, group=1):
    if count <= unroll_to:
        for i in range(count):
            body(i)
    else:
        rounds = count // group

        @pl.loop(0, rounds)
        def _(i):
            for j in range(group):
                body(group * i + j)

        for i in range(rounds * group, count):
            body(i)


NAMES = (
    "a",
    "sx",
    "dx",
    "b0",
    "b1",
    "b2",
    "b3",
    "yl",
    "yr",
    "ryl",
    "ryr",
    "cs",
    "cr",
    "xsl",
    "xsr",
    "xrl",
    "xrr",
    "xfs",
    "xfr",
)


def kernel(levels, counts, x_hbm, w_hbm, out_ref, *scratch):
    count_x, count_y = counts
    (xin, w_ref, mats, temp, in_sem, send_sem, recv_sem) = scratch[:7]
    per = scratch[7:]
    refs = [
        dict(zip(NAMES, per[k * len(NAMES) : (k + 1) * len(NAMES)])) for k in range(LEVELS)
    ]
    gx = lax.axis_index("gx")
    gy = lax.axis_index("gy")
    first_x, last_x = gx == 0, gx == count_x - 1
    planes_in = levels[0].n
    rows_in = levels[0].y
    cells = xin.shape[1] // planes_in

    def at(dx, dy):
        return {
            "gx": lax.rem(gx + dx + count_x, count_x),
            "gy": lax.rem(gy + dy + count_y, count_y),
        }

    friends = [
        (dx, dy) for dx in (-2, -1, 0, 1, 2) for dy in (-1, 0, 1) if (dx, dy) != (0, 0)
    ]
    barrier = pltpu.get_barrier_semaphore()
    for dx, dy in friends:
        pl.semaphore_signal(
            barrier, inc=1, device_id=at(dx, dy), device_id_type=pl.DeviceIdType.MESH
        )
    w_load = pltpu.make_async_copy(w_hbm, w_ref, in_sem.at[2])
    loads = [
        pltpu.make_async_copy(
            x_hbm.at[:, side * rows_in : (side + 1) * rows_in], xin.at[side], in_sem.at[side]
        )
        for side in range(2)
    ]
    for load in loads:
        load.start()
    w_load.start()

    lane = lax.broadcasted_iota(jnp.int32, (1, 128), 1)
    upper = lane >= 64
    keep_next = jnp.logical_or(lane < 64, gy < count_y - 1)
    keep_prev = jnp.logical_or(lane >= 64, gy > 0)
    not_first = jnp.where(first_x, 0.0, 1.0).astype(F32)

    block_row = lax.broadcasted_iota(jnp.int32, (128, 128), 0) // 32
    block_lane = lax.broadcasted_iota(jnp.int32, (128, 128), 1) // 32
    diagonal = block_row == block_lane

    def build(band):
        small = jnp.concatenate([w_ref[band]] * 4, axis=1)
        tiled = jnp.concatenate([small] * 4, axis=0)
        square = jnp.where(diagonal, tiled, 0.0).T
        high = square.astype(BF16)
        low = (square - high.astype(F32)).astype(BF16)
        mats[band, 0:128, 0:128] = high
        mats[band, 128:256, 0:128] = high
        mats[band, 0:128, 128:256] = low
        mats[band, 128:256, 128:256] = jnp.zeros((128, 128), BF16)

    def rows_of(ref, plane, count, row):
        planes, height, _ = ref.shape
        flat = ref.reshape(planes * height, 128)
        return flat, pl.ds(plane * height + row, count, stride=height)

    def gather(ref, plane, count, row):
        flat, where = rows_of(ref, plane, count, row)
        return flat[where, :]

    def scatter(ref, plane, count, row, value):
        flat, where = rows_of(ref, plane, count, row)
        flat[where, :] = value

    top = refs[0]["a"]
    for plane in (0, planes_in + 1, planes_in + 2):
        top[plane] = jnp.zeros(top.shape[1:], F32)
    for row in (7, rows_in + 8, rows_in + 9):
        scatter(top, 1, planes_in, row, jnp.zeros((planes_in, 128), F32))

    edge_right, edge_left = refs[0]["xrr"], refs[0]["xrl"]
    for edge in (edge_right, edge_left):
        for plane in range(edge.shape[0]):
            edge[plane, 0:8] = jnp.zeros((8, 128), F32)
            edge[plane, rows_in + 8 : rows_in + 16] = jnp.zeros((8, 128), F32)

    w_load.wait()

    @pl.loop(0, 4)
    def _(i):
        for j in range(4):
            build(4 * i + j)

    for load in loads:
        load.wait()

    def take(x):
        low = xin[0, pl.ds(x, cells, stride=planes_in), :]
        high = xin[1, pl.ds(x, cells, stride=planes_in), :]
        tile = jnp.concatenate([low, high], axis=0)
        top[x + 1, 8 : 8 + rows_in, :] = tile.T

    def copies(k):
        lv, r = levels[k], refs[k]
        landing = pl.ds(8, rows_in) if lv.first else pl.ds(0, lv.rs)
        moves = [
            (r["xsl"], r["xrr"].at[:, landing], (-1, 0)),
            (r["xsr"], r["xrl"].at[:, landing], (1, 0)),
        ]
        if lv.reach == 2:
            moves.append((r["xfs"].at[0], r["xfr"].at[0], (-2, 0)))
            moves.append((r["xfs"].at[1], r["xfr"].at[1], (2, 0)))
        moves.append((r["yl"], r["ryl"], (0, -1)))
        moves.append((r["yr"], r["ryr"], (0, 1)))
        for i, (hop, way) in enumerate(corners(lv)):
            moves.append((r["cs"].at[i], r["cr"].at[i], (hop, way)))
        ways = {}
        for m, (source, target, way) in enumerate(moves):
            copy = pltpu.make_async_remote_copy(
                src_ref=source,
                dst_ref=target,
                send_sem=send_sem.at[k, m],
                recv_sem=recv_sem.at[k, m],
                device_id=at(*way),
                device_id_type=pl.DeviceIdType.MESH,
            )
            ways.setdefault(way, []).append(copy)
        return ways

    def exists(dx, dy):
        x, y = gx + dx, gy + dy
        inside_x = jnp.logical_and(x >= 0, x < count_x)
        return jnp.logical_and(inside_x, jnp.logical_and(y >= 0, y < count_y))

    def start(ways, wanted):
        for way, group in ways.items():
            if wanted(*way):

                @pl.when(exists(*way))
                def _():
                    for copy in group:
                        copy.start()

    def arrive(ways):
        for (dx, dy), group in ways.items():

            @pl.when(exists(-dx, -dy))
            def _():
                for copy in group:
                    copy.wait_recv()

    def sent(ways):
        for way, group in ways.items():

            @pl.when(exists(*way))
            def _():
                for copy in group:
                    copy.wait_send()

    def send_first():
        n, rows = planes_in, pl.ds(8, rows_in)
        low, high = refs[0]["xsl"], refs[0]["xsr"]
        low[0] = top[1, rows]
        low[1] = top[2, rows] - 0.5 * (top[1, rows] + top[3, rows])
        high[0] = top[n, rows] - 0.5 * top[n - 1, rows]
        start(copies(0), lambda dx, dy: dy == 0)

    def send(k):
        lv, r = levels[k], refs[k]
        todo = copies(k)
        if not lv.first:
            whole, part = slice(7, lv.hy + 10), slice(0, lv.hy + 3)
            for name, low, single in (("xsl", 0, 1), ("xsr", lv.h, lv.h + 1)):
                for i in range(2):
                    r[name][i, part] = r["b1"][low + i, whole]
                    r[name][2 + i, part] = r["b2"][low + i, whole]
                r[name][4, part] = r["b0"][single, whole]
                if lv.last:
                    r[name][5, part] = r["b3"][single, whole]
            if lv.reach == 2:
                for place, plane in ((0, 0), (1, lv.h + 1)):
                    for t in (1, 2):
                        r["xfs"][place, t - 1, part] = r[f"b{t}"][plane, whole]
            start(todo, lambda dx, dy: dy == 0)
        planes = lv.h + 3
        for t, kind in enumerate(lv.kinds):
            for name, hop in (("yl", -1), ("yr", 1)):
                source, _ = lv.y_rows(kind[1], hop)
                for i in range(2):
                    count = planes if kind[0] == "s" else planes - 1
                    value = gather(r[f"b{t}"], 0, count, 8 + source + i)
                    r[name][2 * t + i, 0:count] = value
        for c, (hop, way) in enumerate(corners(lv)):
            strips = r["yl"] if way < 0 else r["yr"]
            for t, kind in enumerate(lv.kinds):
                source, _, count = lv.x_strip(kind[0], hop)
                planes = slice(source + 1, source + 1 + count)
                one, two = strips[2 * t, planes], strips[2 * t + 1, planes]
                if way < 0:
                    both = jnp.where(upper, pltpu.roll(two, 64, 1), one)
                else:
                    both = jnp.where(upper, two, pltpu.roll(one, 64, 1))
                r["cs"][c, 2 * t : 2 * t + count] = both
        start(todo, lambda dx, dy: dy != 0)

    def collect(k):
        lv, r = levels[k], refs[k]
        h = lv.h
        todo = copies(k)
        arrive(todo)
        whole, part = slice(7, lv.hy + 10), slice(0, lv.hy + 3)

        def add(t, position, value):
            r[f"b{t}"][position + 1, whole] = r[f"b{t}"][position + 1, whole] + value

        if lv.first:
            smooth_of = lambda i: temp[2 * i, whole]
            detail_of = lambda i: temp[2 * i + 1, whole]

            lift_y(lv, edge_left.at[0], temp.at[0], temp.at[1], False)
            for i in range(2):
                out = 2 + 2 * i
                lift_y(lv, edge_right.at[i], temp.at[out], temp.at[out + 1], False)
            for c, i in ((gx > 0, 0), (gx < count_x - 1, 1), (gx < count_x - 1, 2)):
                temp[2 * i] = jnp.where(c, temp[2 * i], 0.0)
                temp[2 * i + 1] = jnp.where(c, temp[2 * i + 1], 0.0)
            add(1, -1, smooth_of(0))
            add(2, -1, detail_of(0))
            add(0, 0, 0.25 * detail_of(0))
            add(1, h - 1, -0.5 * smooth_of(1))
            add(2, h - 1, -0.5 * detail_of(1))
            add(1, h, smooth_of(2))
            add(2, h, detail_of(2))
            add(0, h - 1, -0.125 * detail_of(1))
            add(0, h, 0.875 * detail_of(1) + 0.25 * detail_of(2))

        else:
            smooth = [(0, 4, 2)] if lv.bands == 3 else [(0, 4, 2), (3, 5, 0)]
            from_left = lambda i: jnp.where(gx > 0, r["xrl"][i, part], 0.0)
            from_right = lambda i: jnp.where(gx < count_x - 1, r["xrr"][i, part], 0.0)

            for t in (1, 2):
                add(t, -1, from_left(2 * t - 2))
                add(t, 0, from_left(2 * t - 1))
                add(t, h - 1, from_right(2 * t - 2))
                add(t, h, from_right(2 * t - 1))
            for t, slot, d in smooth:
                add(t, 0, from_left(slot))
                add(t, 1, 0.25 * from_left(d + 1))
                add(t, h - 1, 0.25 * from_right(d))
                add(t, h, from_right(slot))

            if lv.reach == 2:
                far = lambda side, d: r["xfr"][side, d, part]

                @pl.when(gx > 1)
                def _():
                    for t in (1, 2):
                        add(t, -1, far(1, t - 1))
                    for t, _, d in smooth:
                        add(t, 0, 0.25 * far(1, d // 2))

                @pl.when(gx < count_x - 2)
                def _():
                    for t in (1, 2):
                        add(t, h, far(0, t - 1))
                    for t, _, d in smooth:
                        add(t, h, 0.25 * far(0, d // 2))

        for c, (hop, way) in enumerate(corners(lv)):
            strips = r["ryl"] if way < 0 else r["ryr"]

            there = exists(-hop, -way)
            for t, kind in enumerate(lv.kinds):
                _, target, count = lv.x_strip(kind[0], hop)
                packed = jnp.where(there, r["cr"][c, 2 * t : 2 * t + count], 0.0)
                other = pltpu.roll(packed, 64, 1)
                planes = slice(target + 1, target + 1 + count)
                for i in range(2):
                    value = packed if (way < 0) == (i == 0) else other
                    strips[2 * t + i, planes] = strips[2 * t + i, planes] + value

        planes = h + 2
        for t, kind in enumerate(lv.kinds):
            band = r[f"b{t}"]
            todo_rows = []
            for i in range(2):
                source, target = lv.y_rows(kind[1], -1)
                here = gather(band, 0, planes, 8 + source + i)
                there = r["ryl"][2 * t + i, 0:planes]
                moved = pltpu.roll(jnp.where(upper, here, there), 64, 1)
                todo_rows.append((target + i, jnp.where(keep_next, moved, 0.0)))
                source, target = lv.y_rows(kind[1], 1)
                here = gather(band, 0, planes, 8 + source + i)
                there = r["ryr"][2 * t + i, 0:planes]
                moved = pltpu.roll(jnp.where(upper, there, here), 64, 1)
                todo_rows.append((target + i, jnp.where(keep_prev, moved, 0.0)))
            for row, value in todo_rows:
                mine = gather(band, 0, planes, 8 + row)
                scatter(band, 0, planes, 8 + row, mine + value)

    def lift_x(k):
        lv = levels[k]
        a, sx, dx = (refs[k][name] for name in ("a", "sx", "dx"))
        n, h = lv.n, lv.h
        low = not_first * (a[0] - 0.5 * a[1])
        dx[0] = low
        sx[0] = 0.25 * low

        def step(i):
            even = a[2 * i + 1]
            detail = a[2 * i + 2] - 0.5 * (even + a[2 * i + 3])
            dx[i + 1] = detail
            sx[i + 1] = even + 0.25 * (dx[i] + detail)

        each(h, step, group=2)
        high = a[n + 2] - 0.5 * a[n + 1]
        dx[h + 1] = high
        sx[h + 1] = a[n + 1] + 0.25 * (dx[h] + high)
        sx[h + 2] = 0.25 * high

    def lift_y(lv, plane, smooth, detail, mask):
        hy, y = lv.hy, lv.y
        even = plane[pl.ds(8, hy, stride=2), :]
        odd = plane[pl.ds(9, hy, stride=2), :]
        after = plane[pl.ds(10, hy, stride=2), :]
        fresh = odd - 0.5 * (even + after)
        detail[8 : 8 + hy] = fresh
        low = jnp.where(keep_prev, plane[7:8] - 0.5 * plane[8:9], 0.0)
        next_even = plane[y + 8 : y + 9]
        high = plane[y + 9 : y + 10] - 0.5 * next_even
        detail[7:8] = low
        detail[8 + hy : 9 + hy] = high
        smooth[8 : 8 + hy] = even + 0.25 * (detail[7 : 7 + hy] + fresh)
        smooth[7:8] = 0.25 * low
        end = next_even + 0.25 * (detail[7 + hy : 8 + hy] + high)
        end_next = 0.25 * high
        if mask:
            end = jnp.where(keep_next, end, 0.0)
            end_next = jnp.where(keep_next, end_next, 0.0)
        smooth[8 + hy : 9 + hy] = end
        smooth[9 + hy : 10 + hy] = end_next

    def lift_smooth(k):
        lv, r = levels[k], refs[k]
        coarse = r["b3"] if lv.last else refs[k + 1]["a"]
        each(
            lv.h + 3,
            lambda i: lift_y(lv, r["sx"].at[i], coarse.at[i], r["b0"].at[i], not lv.last),
            group=3,
        )
        if not lv.last:

            @pl.when(last_x)
            def _():
                coarse[lv.h + 1] = jnp.zeros_like(coarse[lv.h + 1])
                coarse[lv.h + 2] = jnp.zeros_like(coarse[lv.h + 2])

    def lift_detail(k):
        lv, r = levels[k], refs[k]
        each(
            lv.h + 2,
            lambda i: lift_y(lv, r["dx"].at[i], r["b1"].at[i], r["b2"].at[i], False),
            group=3,
        )

    def weigh(ref, band, begin, planes, most=512):
        rows = ref.shape[1]
        chunk = planes
        while chunk * rows > most and chunk % 3 == 0:
            chunk //= 3

        def step(i):
            part = pl.ds(begin + i * chunk, chunk)
            value = ref[part].reshape(chunk * rows, 128)
            high = value.astype(BF16)
            low = (value - high.astype(F32)).astype(BF16)
            both = jnp.concatenate([high, low], axis=1)
            product = jnp.dot(both, mats[band], preferred_element_type=F32)
            total = product[:, :128] + product[:, 128:]
            ref[part] = total.reshape(chunk, rows, 128)

        each(planes // chunk, step, 1)

    def weigh_bands(k):
        lv, r = levels[k], refs[k]
        for t in range(lv.bands):
            weigh(r[f"b{t}"], 3 * k + t, 0, lv.h + 2)

    def unlift_y(lv, smooth, detail, plane):
        hy, y = lv.hy, lv.y
        fresh = detail[8 : 8 + hy]
        even = smooth[8 : 8 + hy] - 0.25 * (detail[7 : 7 + hy] + fresh)
        plane[pl.ds(8, hy, stride=2), :] = even
        last = smooth[8 + hy : 9 + hy] - 0.25 * (
            detail[7 + hy : 8 + hy] + detail[8 + hy : 9 + hy]
        )
        plane[y + 8 : y + 9] = jnp.where(keep_next, last, 0.0)
        after = plane[pl.ds(10, hy, stride=2), :]
        plane[pl.ds(9, hy, stride=2), :] = fresh + 0.5 * (even + after)

    def unlift_detail(k):
        lv, r = levels[k], refs[k]
        each(
            lv.h + 2,
            lambda i: unlift_y(lv, r["b1"].at[i], r["b2"].at[i], r["dx"].at[i]),
            group=3,
        )

    def unlift_smooth(k, coarse):
        lv, r = levels[k], refs[k]
        each(
            lv.h + 1,
            lambda i: unlift_y(lv, coarse.at[i + 1], r["b0"].at[i + 1], r["sx"].at[i + 1]),
            group=3,
        )

    def unlift_x(k, target, emit=None):
        lv = levels[k]
        sx, dx = refs[k]["sx"], refs[k]["dx"]
        n, h = lv.n, lv.h
        target[1] = sx[1] - 0.25 * (dx[0] + dx[1])

        @pl.when(jnp.logical_not(last_x))
        def _():
            target[n + 1] = sx[h + 1] - 0.25 * (dx[h] + dx[h + 1])

        @pl.when(last_x)
        def _():
            target[n + 1] = jnp.zeros_like(target[n + 1])

        def step(i):
            even = target[2 * i + 1]
            middle = dx[i + 1]
            after = sx[i + 2] - 0.25 * (middle + dx[i + 2])
            target[2 * i + 3] = after
            odd = middle + 0.5 * (even + after)
            target[2 * i + 2] = odd
            if emit is not None:
                emit(2 * i, even)
                emit(2 * i + 1, odd)

        each(h - 1, step, group=3)
        even, after, middle = target[n - 1], target[n + 1], dx[h]
        odd = middle + 0.5 * (even + after)
        target[n] = odd
        if emit is not None:
            emit(n - 2, even)
            emit(n - 1, odd)

    edge_planes = (0, 1, 2, planes_in - 2, planes_in - 1)
    for x in edge_planes:
        take(x)
    @pl.loop(0, (planes_in - len(edge_planes)) // 3)
    def _(i):
        for j in range(3):
            take(3 + 3 * i + j)

    pl.semaphore_wait(barrier, len(friends))
    send_first()

    for k in range(LEVELS):
        lift_x(k)
        lift_smooth(k)
        lift_detail(k)
        send(k)
    for k in range(LEVELS):
        collect(k)
        weigh_bands(k)
        unlift_detail(k)

    def emit(x, value):
        tile = value[8 : 8 + rows_in].T
        base = (x // 8) * 16 + lax.rem(x, 8)
        out_ref[pl.ds(base, cells, stride=2 * planes_in), :] = tile[:cells]
        out_ref[pl.ds(base + 8, cells, stride=2 * planes_in), :] = tile[cells:]

    coarse = refs[LEVELS - 1]["b3"]
    for k in reversed(range(LEVELS)):
        unlift_smooth(k, coarse)
        coarse = refs[k]["a"]
        unlift_x(k, coarse, emit if k == 0 else None)
    for k in range(LEVELS):
        sent(copies(k))


def corners(lv):
    hops = [-1, 1] + ([-2, 2] if lv.reach == 2 else [])
    return [(hop, way) for way in (-1, 1) for hop in hops]


def per_device(counts, control, band_roots):
    vectors, layers, planes, cols = control.shape
    rows = cols // 2
    levels = levels_of(planes, rows)
    cells = vectors * layers
    x = control.reshape(cells * planes, cols)
    scratch = [
        pltpu.VMEM((2, cells * planes, rows), F32),
        pltpu.VMEM(band_roots.shape, F32),
        pltpu.VMEM((16, 256, 256), BF16),
        pltpu.VMEM((6, levels[0].rb, 128), F32),
        pltpu.SemaphoreType.DMA((3,)),
        pltpu.SemaphoreType.DMA((LEVELS, 24)),
        pltpu.SemaphoreType.DMA((LEVELS, 24)),
    ]
    for lv in levels:
        t, h = lv.bands, lv.h
        shapes = dict(
            a=(lv.n + 3, lv.r),
            sx=(h + 3, lv.r),
            dx=(h + 2, lv.r),
            b0=(h + 3, lv.rb),
            b1=(h + 2, lv.rb),
            b2=(h + 2, lv.rb),
            b3=(h + 3, lv.rb),
            yl=(2 * t, lv.hp),
            yr=(2 * t, lv.hp),
            ryl=(2 * t, lv.hp),
            ryr=(2 * t, lv.hp),
            cs=(len(corners(lv)), 8),
            cr=(len(corners(lv)), 8),
            xsl=(2, lv.y) if lv.first else (t + 2, lv.rs),
            xsr=(1, lv.y) if lv.first else (t + 2, lv.rs),
            xrl=(1, lv.y + 16) if lv.first else (t + 2, lv.rs),
            xrr=(2, lv.y + 16) if lv.first else (t + 2, lv.rs),
            xfs=(2, 2, lv.rs),
            xfr=(2, 2, lv.rs),
        )
        for name in NAMES:
            used = {"b3": lv.last, "xfs": lv.last, "xfr": lv.last}.get(name, True)
            scratch.append(pltpu.VMEM((shapes[name] if used else (8,)) + (128,), F32))
    out = pl.pallas_call(
        partial(kernel, levels, counts),
        out_shape=jax.ShapeDtypeStruct((cells * planes * 2, rows), F32),
        in_specs=[
            pl.BlockSpec(memory_space=pltpu.HBM),
            pl.BlockSpec(memory_space=pltpu.HBM),
        ],
        out_specs=pl.BlockSpec(memory_space=pltpu.VMEM),
        scratch_shapes=scratch,
        compiler_params=pltpu.CompilerParams(
            collective_id=0, has_side_effects=True, vmem_limit_bytes=54000000
        ),
        name="wavelet",
    )(x, band_roots)
    out = out.reshape(cells * planes // 8, 2, 8, rows).transpose(0, 2, 1, 3)
    return out.reshape(control.shape)


def solution(mesh):
    counts = (mesh.shape["gx"], mesh.shape["gy"])
    in_specs = (P(None, None, "gx", "gy"), P())
    out_specs = P(None, None, "gx", "gy")
    return jax.shard_map(
        partial(per_device, counts),
        mesh=mesh,
        in_specs=in_specs,
        out_specs=out_specs,
        check_vma=False,
    )
```

```python
from functools import partial

import jax
import jax.numpy as jnp
from jax import lax
from jax.experimental import pallas as pl
from jax.experimental.pallas import tpu as pltpu
from jax.sharding import PartitionSpec as P

LEVELS = 5
F32 = jnp.float32
BF16 = jnp.bfloat16


def round_up(value, step):
    return (value + step - 1) // step * step


class Level:
    def __init__(self, planes, rows, first, last):
        self.n = planes
        self.y = rows
        self.h = planes // 2
        self.hy = rows // 2
        self.first = first
        self.last = last
        self.r = round_up(rows + 10, 8)
        self.rb = round_up(self.hy + 10, 16)
        self.rs = round_up(self.hy + 3, 8)
        self.hp = round_up(self.h + 3, 8)
        self.bands = 4 if last else 3
        self.kinds = ["sd", "ds", "dd", "ss"][: self.bands]
        self.reach = 2 if self.h == 1 else 1

    def x_strip(self, kind, hop):
        low = -1 if kind == "d" else 0
        high = self.h + (1 if kind == "s" else 0)
        begin = max(low, -1 - hop * self.h)
        end = min(self.h, high - hop * self.h)
        return begin + hop * self.h, begin, end - begin + 1

    def y_rows(self, kind, hop):
        if hop < 0:
            return -1, self.hy - 1
        return (self.hy - 1, -1) if kind == "d" else (self.hy, 0)


def levels_of(planes, rows):
    return [
        Level(planes >> k, rows >> k, k == 0, k == LEVELS - 1) for k in range(LEVELS)
    ]


def each(count, body, unroll_to=4, group=1):
    if count <= unroll_to:
        for i in range(count):
            body(i)
    else:
        rounds = count // group

        @pl.loop(0, rounds)
        def _(i):
            for j in range(group):
                body(group * i + j)

        for i in range(rounds * group, count):
            body(i)


NAMES = (
    "a",
    "sx",
    "dx",
    "b0",
    "b1",
    "b2",
    "b3",
    "yl",
    "yr",
    "ryl",
    "ryr",
    "cs",
    "cr",
    "xsl",
    "xsr",
    "xrl",
    "xrr",
    "xfs",
    "xfr",
)


def kernel(levels, counts, x_hbm, w_hbm, out_ref, *scratch):
    count_x, count_y = counts
    (xin, w_ref, mats, temp, in_sem, send_sem, recv_sem) = scratch[:7]
    per = scratch[7:]
    refs = [
        dict(zip(NAMES, per[k * len(NAMES) : (k + 1) * len(NAMES)])) for k in range(LEVELS)
    ]
    gx = lax.axis_index("gx")
    gy = lax.axis_index("gy")
    first_x, last_x = gx == 0, gx == count_x - 1
    planes_in = levels[0].n
    rows_in = levels[0].y
    cells = xin.shape[1] // planes_in

    def at(dx, dy):
        return {
            "gx": lax.rem(gx + dx + count_x, count_x),
            "gy": lax.rem(gy + dy + count_y, count_y),
        }

    def exists(dx, dy):
        x, y = gx + dx, gy + dy
        inside_x = jnp.logical_and(x >= 0, x < count_x)
        return jnp.logical_and(inside_x, jnp.logical_and(y >= 0, y < count_y))

    friends = [
        (dx, dy) for dx in (-2, -1, 0, 1, 2) for dy in (-1, 0, 1) if (dx, dy) != (0, 0)
    ]
    barrier = pltpu.get_barrier_semaphore()
    for dx, dy in friends:

        @pl.when(exists(dx, dy))
        def _():
            pl.semaphore_signal(
                barrier, inc=1, device_id=at(dx, dy), device_id_type=pl.DeviceIdType.MESH
            )

    w_load = pltpu.make_async_copy(w_hbm, w_ref, in_sem.at[2])
    loads = [
        pltpu.make_async_copy(
            x_hbm.at[:, side * rows_in : (side + 1) * rows_in], xin.at[side], in_sem.at[side]
        )
        for side in range(2)
    ]
    for load in loads:
        load.start()
    w_load.start()

    lane = lax.broadcasted_iota(jnp.int32, (1, 128), 1)
    upper = lane >= 64
    keep_next = jnp.logical_or(lane < 64, gy < count_y - 1)
    keep_prev = jnp.logical_or(lane >= 64, gy > 0)
    not_first = jnp.where(first_x, 0.0, 1.0).astype(F32)

    block_row = lax.broadcasted_iota(jnp.int32, (128, 128), 0) // 32
    block_lane = lax.broadcasted_iota(jnp.int32, (128, 128), 1) // 32
    diagonal = block_row == block_lane

    def build(band):
        small = jnp.concatenate([w_ref[band]] * 4, axis=1)
        tiled = jnp.concatenate([small] * 4, axis=0)
        square = jnp.where(diagonal, tiled, 0.0).T
        high = square.astype(BF16)
        low = (square - high.astype(F32)).astype(BF16)
        mats[band, 0:128, 0:128] = high
        mats[band, 128:256, 0:128] = high
        mats[band, 0:128, 128:256] = low
        mats[band, 128:256, 128:256] = jnp.zeros((128, 128), BF16)

    def rows_of(ref, plane, count, row):
        planes, height, _ = ref.shape
        flat = ref.reshape(planes * height, 128)
        return flat, pl.ds(plane * height + row, count, stride=height)

    def gather(ref, plane, count, row):
        flat, where = rows_of(ref, plane, count, row)
        return flat[where, :]

    def scatter(ref, plane, count, row, value):
        flat, where = rows_of(ref, plane, count, row)
        flat[where, :] = value

    top = refs[0]["a"]
    for plane in (0, planes_in + 1, planes_in + 2):
        top[plane] = jnp.zeros(top.shape[1:], F32)
    for row in (7, rows_in + 8, rows_in + 9):
        scatter(top, 1, planes_in, row, jnp.zeros((planes_in, 128), F32))

    edge_right, edge_left = refs[0]["xrr"], refs[0]["xrl"]
    for edge in (edge_right, edge_left):
        for plane in range(edge.shape[0]):
            edge[plane, 0:8] = jnp.zeros((8, 128), F32)
            edge[plane, rows_in + 8 : rows_in + 16] = jnp.zeros((8, 128), F32)

    w_load.wait()

    @pl.loop(0, 4)
    def _(i):
        for j in range(4):
            build(4 * i + j)

    for load in loads:
        load.wait()

    def take(x):
        low = xin[0, pl.ds(x, cells, stride=planes_in), :]
        high = xin[1, pl.ds(x, cells, stride=planes_in), :]
        tile = jnp.concatenate([low, high], axis=0)
        top[x + 1, 8 : 8 + rows_in, :] = tile.T

    def copies(k):
        lv, r = levels[k], refs[k]
        landing = pl.ds(8, rows_in) if lv.first else pl.ds(0, lv.rs)
        moves = [
            (r["xsl"], r["xrr"].at[:, landing], (-1, 0)),
            (r["xsr"], r["xrl"].at[:, landing], (1, 0)),
        ]
        if lv.reach == 2:
            moves.append((r["xfs"].at[0], r["xfr"].at[0], (-2, 0)))
            moves.append((r["xfs"].at[1], r["xfr"].at[1], (2, 0)))
        moves.append((r["yl"], r["ryl"], (0, -1)))
        moves.append((r["yr"], r["ryr"], (0, 1)))
        for i, (hop, way) in enumerate(corners(lv)):
            moves.append((r["cs"].at[i], r["cr"].at[i], (hop, way)))
        ways = {}
        for m, (source, target, way) in enumerate(moves):
            copy = pltpu.make_async_remote_copy(
                src_ref=source,
                dst_ref=target,
                send_sem=send_sem.at[k, m],
                recv_sem=recv_sem.at[k, m],
                device_id=at(*way),
                device_id_type=pl.DeviceIdType.MESH,
            )
            ways.setdefault(way, []).append(copy)
        return ways

    def start(ways, wanted):
        for way, group in ways.items():
            if wanted(*way):

                @pl.when(exists(*way))
                def _():
                    for copy in group:
                        copy.start()

    def arrive(ways):
        for (dx, dy), group in ways.items():

            @pl.when(exists(-dx, -dy))
            def _():
                for copy in group:
                    copy.wait_recv()

    def sent(ways):
        for way, group in ways.items():

            @pl.when(exists(*way))
            def _():
                for copy in group:
                    copy.wait_send()

    def send_first():
        n, rows = planes_in, pl.ds(8, rows_in)
        low, high = refs[0]["xsl"], refs[0]["xsr"]
        low[0] = top[1, rows]
        low[1] = top[2, rows] - 0.5 * (top[1, rows] + top[3, rows])
        high[0] = top[n, rows] - 0.5 * top[n - 1, rows]
        start(copies(0), lambda dx, dy: dy == 0)

    def send(k):
        lv, r = levels[k], refs[k]
        todo = copies(k)
        if not lv.first:
            whole, part = slice(7, lv.hy + 10), slice(0, lv.hy + 3)
            for name, low, single in (("xsl", 0, 1), ("xsr", lv.h, lv.h + 1)):
                for i in range(2):
                    r[name][i, part] = r["b1"][low + i, whole]
                    r[name][2 + i, part] = r["b2"][low + i, whole]
                r[name][4, part] = r["b0"][single, whole]
                if lv.last:
                    r[name][5, part] = r["b3"][single, whole]
            if lv.reach == 2:
                for place, plane in ((0, 0), (1, lv.h + 1)):
                    for t in (1, 2):
                        r["xfs"][place, t - 1, part] = r[f"b{t}"][plane, whole]
            start(todo, lambda dx, dy: dy == 0)
        planes = lv.h + 3
        for t, kind in enumerate(lv.kinds):
            for name, hop in (("yl", -1), ("yr", 1)):
                source, _ = lv.y_rows(kind[1], hop)
                for i in range(2):
                    count = planes if kind[0] == "s" else planes - 1
                    value = gather(r[f"b{t}"], 0, count, 8 + source + i)
                    r[name][2 * t + i, 0:count] = value
        for c, (hop, way) in enumerate(corners(lv)):
            strips = r["yl"] if way < 0 else r["yr"]
            for t, kind in enumerate(lv.kinds):
                source, _, count = lv.x_strip(kind[0], hop)
                planes = slice(source + 1, source + 1 + count)
                one, two = strips[2 * t, planes], strips[2 * t + 1, planes]
                if way < 0:
                    both = jnp.where(upper, pltpu.roll(two, 64, 1), one)
                else:
                    both = jnp.where(upper, two, pltpu.roll(one, 64, 1))
                r["cs"][c, 2 * t : 2 * t + count] = both
        start(todo, lambda dx, dy: dy != 0)

    def collect(k):
        lv, r = levels[k], refs[k]
        h = lv.h
        todo = copies(k)
        arrive(todo)
        whole, part = slice(7, lv.hy + 10), slice(0, lv.hy + 3)

        def add(t, position, value):
            r[f"b{t}"][position + 1, whole] = r[f"b{t}"][position + 1, whole] + value

        if lv.first:
            smooth_of = lambda i: temp[2 * i, whole]
            detail_of = lambda i: temp[2 * i + 1, whole]

            lift_y(lv, edge_left.at[0], temp.at[0], temp.at[1], False)
            for i in range(2):
                out = 2 + 2 * i
                lift_y(lv, edge_right.at[i], temp.at[out], temp.at[out + 1], False)
            for c, i in ((gx > 0, 0), (gx < count_x - 1, 1), (gx < count_x - 1, 2)):
                temp[2 * i] = jnp.where(c, temp[2 * i], 0.0)
                temp[2 * i + 1] = jnp.where(c, temp[2 * i + 1], 0.0)
            add(1, -1, smooth_of(0))
            add(2, -1, detail_of(0))
            add(0, 0, 0.25 * detail_of(0))
            add(1, h - 1, -0.5 * smooth_of(1))
            add(2, h - 1, -0.5 * detail_of(1))
            add(1, h, smooth_of(2))
            add(2, h, detail_of(2))
            add(0, h - 1, -0.125 * detail_of(1))
            add(0, h, 0.875 * detail_of(1) + 0.25 * detail_of(2))

        else:
            smooth = [(0, 4, 2)] if lv.bands == 3 else [(0, 4, 2), (3, 5, 0)]
            from_left = lambda i: jnp.where(gx > 0, r["xrl"][i, part], 0.0)
            from_right = lambda i: jnp.where(gx < count_x - 1, r["xrr"][i, part], 0.0)

            for t in (1, 2):
                add(t, -1, from_left(2 * t - 2))
                add(t, 0, from_left(2 * t - 1))
                add(t, h - 1, from_right(2 * t - 2))
                add(t, h, from_right(2 * t - 1))
            for t, slot, d in smooth:
                add(t, 0, from_left(slot))
                add(t, 1, 0.25 * from_left(d + 1))
                add(t, h - 1, 0.25 * from_right(d))
                add(t, h, from_right(slot))

            if lv.reach == 2:
                far = lambda side, d: r["xfr"][side, d, part]

                @pl.when(gx > 1)
                def _():
                    for t in (1, 2):
                        add(t, -1, far(1, t - 1))
                    for t, _, d in smooth:
                        add(t, 0, 0.25 * far(1, d // 2))

                @pl.when(gx < count_x - 2)
                def _():
                    for t in (1, 2):
                        add(t, h, far(0, t - 1))
                    for t, _, d in smooth:
                        add(t, h, 0.25 * far(0, d // 2))

        for c, (hop, way) in enumerate(corners(lv)):
            strips = r["ryl"] if way < 0 else r["ryr"]

            there = exists(-hop, -way)
            for t, kind in enumerate(lv.kinds):
                _, target, count = lv.x_strip(kind[0], hop)
                packed = jnp.where(there, r["cr"][c, 2 * t : 2 * t + count], 0.0)
                other = pltpu.roll(packed, 64, 1)
                planes = slice(target + 1, target + 1 + count)
                for i in range(2):
                    value = packed if (way < 0) == (i == 0) else other
                    strips[2 * t + i, planes] = strips[2 * t + i, planes] + value

        planes = h + 2
        for t, kind in enumerate(lv.kinds):
            band = r[f"b{t}"]
            todo_rows = []
            for i in range(2):
                source, target = lv.y_rows(kind[1], -1)
                here = gather(band, 0, planes, 8 + source + i)
                there = r["ryl"][2 * t + i, 0:planes]
                moved = pltpu.roll(jnp.where(upper, here, there), 64, 1)
                todo_rows.append((target + i, jnp.where(keep_next, moved, 0.0)))
                source, target = lv.y_rows(kind[1], 1)
                here = gather(band, 0, planes, 8 + source + i)
                there = r["ryr"][2 * t + i, 0:planes]
                moved = pltpu.roll(jnp.where(upper, there, here), 64, 1)
                todo_rows.append((target + i, jnp.where(keep_prev, moved, 0.0)))
            for row, value in todo_rows:
                mine = gather(band, 0, planes, 8 + row)
                scatter(band, 0, planes, 8 + row, mine + value)

    def lift_x(k):
        lv = levels[k]
        a, sx, dx = (refs[k][name] for name in ("a", "sx", "dx"))
        n, h = lv.n, lv.h
        low = not_first * (a[0] - 0.5 * a[1])
        dx[0] = low
        sx[0] = 0.25 * low

        def step(i):
            even = a[2 * i + 1]
            detail = a[2 * i + 2] - 0.5 * (even + a[2 * i + 3])
            dx[i + 1] = detail
            sx[i + 1] = even + 0.25 * (dx[i] + detail)

        each(h, step, group=2)
        high = a[n + 2] - 0.5 * a[n + 1]
        dx[h + 1] = high
        sx[h + 1] = a[n + 1] + 0.25 * (dx[h] + high)
        sx[h + 2] = 0.25 * high

    def lift_y(lv, plane, smooth, detail, mask):
        hy, y = lv.hy, lv.y
        even = plane[pl.ds(8, hy, stride=2), :]
        odd = plane[pl.ds(9, hy, stride=2), :]
        after = plane[pl.ds(10, hy, stride=2), :]
        fresh = odd - 0.5 * (even + after)
        detail[8 : 8 + hy] = fresh
        low = jnp.where(keep_prev, plane[7:8] - 0.5 * plane[8:9], 0.0)
        next_even = plane[y + 8 : y + 9]
        high = plane[y + 9 : y + 10] - 0.5 * next_even
        detail[7:8] = low
        detail[8 + hy : 9 + hy] = high
        smooth[8 : 8 + hy] = even + 0.25 * (detail[7 : 7 + hy] + fresh)
        smooth[7:8] = 0.25 * low
        end = next_even + 0.25 * (detail[7 + hy : 8 + hy] + high)
        end_next = 0.25 * high
        if mask:
            end = jnp.where(keep_next, end, 0.0)
            end_next = jnp.where(keep_next, end_next, 0.0)
        smooth[8 + hy : 9 + hy] = end
        smooth[9 + hy : 10 + hy] = end_next

    def lift_smooth(k):
        lv, r = levels[k], refs[k]
        coarse = r["b3"] if lv.last else refs[k + 1]["a"]
        each(
            lv.h + 3,
            lambda i: lift_y(lv, r["sx"].at[i], coarse.at[i], r["b0"].at[i], not lv.last),
            group=3,
        )
        if not lv.last:

            @pl.when(last_x)
            def _():
                coarse[lv.h + 1] = jnp.zeros_like(coarse[lv.h + 1])
                coarse[lv.h + 2] = jnp.zeros_like(coarse[lv.h + 2])

    def lift_detail(k):
        lv, r = levels[k], refs[k]
        each(
            lv.h + 2,
            lambda i: lift_y(lv, r["dx"].at[i], r["b1"].at[i], r["b2"].at[i], False),
            group=3,
        )

    def weigh(ref, band, begin, planes, most=512):
        rows = ref.shape[1]
        chunk = planes
        while chunk * rows > most and chunk % 3 == 0:
            chunk //= 3

        def step(i):
            part = pl.ds(begin + i * chunk, chunk)
            value = ref[part].reshape(chunk * rows, 128)
            high = value.astype(BF16)
            low = (value - high.astype(F32)).astype(BF16)
            both = jnp.concatenate([high, low], axis=1)
            product = jnp.dot(both, mats[band], preferred_element_type=F32)
            total = product[:, :128] + product[:, 128:]
            ref[part] = total.reshape(chunk, rows, 128)

        each(planes // chunk, step, 1)

    def weigh_bands(k):
        lv, r = levels[k], refs[k]
        for t in range(lv.bands):
            weigh(r[f"b{t}"], 3 * k + t, 0, lv.h + 2)

    def unlift_y(lv, smooth, detail, plane):
        hy, y = lv.hy, lv.y
        fresh = detail[8 : 8 + hy]
        even = smooth[8 : 8 + hy] - 0.25 * (detail[7 : 7 + hy] + fresh)
        plane[pl.ds(8, hy, stride=2), :] = even
        last = smooth[8 + hy : 9 + hy] - 0.25 * (
            detail[7 + hy : 8 + hy] + detail[8 + hy : 9 + hy]
        )
        plane[y + 8 : y + 9] = jnp.where(keep_next, last, 0.0)
        after = plane[pl.ds(10, hy, stride=2), :]
        plane[pl.ds(9, hy, stride=2), :] = fresh + 0.5 * (even + after)

    def unlift_detail(k):
        lv, r = levels[k], refs[k]
        each(
            lv.h + 2,
            lambda i: unlift_y(lv, r["b1"].at[i], r["b2"].at[i], r["dx"].at[i]),
            group=3,
        )

    def unlift_smooth(k, coarse):
        lv, r = levels[k], refs[k]
        each(
            lv.h + 1,
            lambda i: unlift_y(lv, coarse.at[i + 1], r["b0"].at[i + 1], r["sx"].at[i + 1]),
            group=3,
        )

    def unlift_x(k, target, emit=None):
        lv = levels[k]
        sx, dx = refs[k]["sx"], refs[k]["dx"]
        n, h = lv.n, lv.h
        target[1] = sx[1] - 0.25 * (dx[0] + dx[1])

        @pl.when(jnp.logical_not(last_x))
        def _():
            target[n + 1] = sx[h + 1] - 0.25 * (dx[h] + dx[h + 1])

        @pl.when(last_x)
        def _():
            target[n + 1] = jnp.zeros_like(target[n + 1])

        def step(i):
            even = target[2 * i + 1]
            middle = dx[i + 1]
            after = sx[i + 2] - 0.25 * (middle + dx[i + 2])
            target[2 * i + 3] = after
            odd = middle + 0.5 * (even + after)
            target[2 * i + 2] = odd
            if emit is not None:
                emit(2 * i, even)
                emit(2 * i + 1, odd)

        each(h - 1, step, group=3)
        even, after, middle = target[n - 1], target[n + 1], dx[h]
        odd = middle + 0.5 * (even + after)
        target[n] = odd
        if emit is not None:
            emit(n - 2, even)
            emit(n - 1, odd)

    edge_planes = (0, 1, 2, planes_in - 2, planes_in - 1)
    for x in edge_planes:
        take(x)
    @pl.loop(0, (planes_in - len(edge_planes)) // 3)
    def _(i):
        for j in range(3):
            take(3 + 3 * i + j)

    peers = sum(jnp.where(exists(dx, dy), 1, 0) for dx, dy in friends)
    pl.semaphore_wait(barrier, peers)
    send_first()

    for k in range(LEVELS):
        lift_x(k)
        lift_smooth(k)
        lift_detail(k)
        send(k)
    for k in range(LEVELS):
        collect(k)
        weigh_bands(k)
        unlift_detail(k)

    def emit(x, value):
        tile = value[8 : 8 + rows_in].T
        base = (x // 8) * 16 + lax.rem(x, 8)
        out_ref[pl.ds(base, cells, stride=2 * planes_in), :] = tile[:cells]
        out_ref[pl.ds(base + 8, cells, stride=2 * planes_in), :] = tile[cells:]

    coarse = refs[LEVELS - 1]["b3"]
    for k in reversed(range(LEVELS)):
        unlift_smooth(k, coarse)
        coarse = refs[k]["a"]
        unlift_x(k, coarse, emit if k == 0 else None)
    for k in range(LEVELS):
        sent(copies(k))


def corners(lv):
    hops = [-1, 1] + ([-2, 2] if lv.reach == 2 else [])
    return [(hop, way) for way in (-1, 1) for hop in hops]


def per_device(counts, control, band_roots):
    vectors, layers, planes, cols = control.shape
    rows = cols // 2
    levels = levels_of(planes, rows)
    cells = vectors * layers
    x = control.reshape(cells * planes, cols)
    scratch = [
        pltpu.VMEM((2, cells * planes, rows), F32),
        pltpu.VMEM(band_roots.shape, F32),
        pltpu.VMEM((16, 256, 256), BF16),
        pltpu.VMEM((6, levels[0].rb, 128), F32),
        pltpu.SemaphoreType.DMA((3,)),
        pltpu.SemaphoreType.DMA((LEVELS, 24)),
        pltpu.SemaphoreType.DMA((LEVELS, 24)),
    ]
    for lv in levels:
        t, h = lv.bands, lv.h
        shapes = dict(
            a=(lv.n + 3, lv.r),
            sx=(h + 3, lv.r),
            dx=(h + 2, lv.r),
            b0=(h + 3, lv.rb),
            b1=(h + 2, lv.rb),
            b2=(h + 2, lv.rb),
            b3=(h + 3, lv.rb),
            yl=(2 * t, lv.hp),
            yr=(2 * t, lv.hp),
            ryl=(2 * t, lv.hp),
            ryr=(2 * t, lv.hp),
            cs=(len(corners(lv)), 8),
            cr=(len(corners(lv)), 8),
            xsl=(2, lv.y) if lv.first else (t + 2, lv.rs),
            xsr=(1, lv.y) if lv.first else (t + 2, lv.rs),
            xrl=(1, lv.y + 16) if lv.first else (t + 2, lv.rs),
            xrr=(2, lv.y + 16) if lv.first else (t + 2, lv.rs),
            xfs=(2, 2, lv.rs),
            xfr=(2, 2, lv.rs),
        )
        for name in NAMES:
            used = {"b3": lv.last, "xfs": lv.last, "xfr": lv.last}.get(name, True)
            scratch.append(pltpu.VMEM((shapes[name] if used else (8,)) + (128,), F32))
    out = pl.pallas_call(
        partial(kernel, levels, counts),
        out_shape=jax.ShapeDtypeStruct((cells * planes * 2, rows), F32),
        in_specs=[
            pl.BlockSpec(memory_space=pltpu.HBM),
            pl.BlockSpec(memory_space=pltpu.HBM),
        ],
        out_specs=pl.BlockSpec(memory_space=pltpu.VMEM),
        scratch_shapes=scratch,
        compiler_params=pltpu.CompilerParams(
            collective_id=0, has_side_effects=True, vmem_limit_bytes=54000000
        ),
        name="wavelet",
    )(x, band_roots)
    out = out.reshape(cells * planes // 8, 2, 8, rows).transpose(0, 2, 1, 3)
    return out.reshape(control.shape)


def solution(mesh):
    counts = (mesh.shape["gx"], mesh.shape["gy"])
    in_specs = (P(None, None, "gx", "gy"), P())
    out_specs = P(None, None, "gx", "gy")
    return jax.shard_map(
        partial(per_device, counts),
        mesh=mesh,
        in_specs=in_specs,
        out_specs=out_specs,
        check_vma=False,
    )
```
